32 devices in a mesh: dom: 2 (over x), frame: 16 (over z, y, core).
Axes of the slice: x: 2, y: 2, z: 4, core: 2. Of those that a mesh axis runs over, the one named last changes fastest.
Arguments:
- queries: bfloat16 [32, 512, 1024], P(('dom', 'frame')), parts along dimension 0, may hold values from -8 to 8
- keys: bfloat16 [32, 512, 1024], P(('dom', 'frame')), parts along dimension 0, may hold values from -8 to 8
- values: bfloat16 [32, 512, 1024], P(('dom', 'frame')), parts along dimension 0, may hold values from -6 to 6
- grad_out: bfloat16 [32, 512, 1024], P(('dom', 'frame')), parts along dimension 0, may hold values from -6 to 6
- links: int32 [32, 4], P(('dom', 'frame')), parts along dimension 0, may hold values from 0 to 1, as said below
- w_query: bfloat16 [1024, 1024], replicated, may hold values from -0.1875 to 0.1875
- w_key: bfloat16 [1024, 1024], replicated, may hold values from -0.1875 to 0.1875
- w_value: bfloat16 [1024, 1024], replicated, may hold values from -0.1875 to 0.1875
Outputs:
- grad_input: bfloat16 [32, 512, 1024], P(('dom', 'frame')), parts along dimension 0
The draws below stay inside these ranges and needn't reach their ends.
There are 2 independent parts, one for each index of `dom`. The reference program is written for one: setup_inputs(seed, part) draws one part's arguments, and reference() takes and returns one part's arrays. A program takes and returns all parts, laid end to end along the dimension named above; an argument that names none is the same for every part. Nothing has to cross between parts.
Inputs may be any that keep to these rules, and one draw needn't show every extreme that they name: links[t, j] is 0 whenever t < 2**j; otherwise 0 or 1, so frames attend to ragged numbers of up to 4 earlier frames.
All inputs are finite; a program needn't handle non-finite values.
Results may differ from the reference program's by a relative error of at most 0.0049.
Values may be sent and summed in bfloat16 or wider, within the bound.
A program may use at most 128 MiB of HBM per device.

```python
import jax
import jax.numpy as jnp
from jax import lax

D = 1024
HEADS = 16
PATCH = 512
NDIL = 4
FRAMES = 16


def base_draw(key, salt_value):
    sub_key = jax.random.fold_in(key, salt_value)
    return jnp.clip(jax.random.normal(sub_key, (FRAMES, PATCH, D), jnp.float32), -6.0, 6.0)


def draw_queries(key, part):
    base_field = base_draw(key, 1)
    return base_field.astype(jnp.bfloat16)


def draw_keys(key, part):
    base_field = base_draw(key, 2)
    return base_field.astype(jnp.bfloat16)


def draw_links(key, part):
    link_bits = jax.random.randint(jax.random.fold_in(key, 3), (FRAMES, NDIL), 0, 4)
    frame_ids = lax.broadcasted_iota(jnp.int32, (FRAMES, NDIL), 0)
    columns = lax.broadcasted_iota(jnp.int32, (FRAMES, NDIL), 1)
    spacings = jnp.left_shift(jnp.ones((FRAMES, NDIL), jnp.int32), columns)
    return jnp.where((link_bits > 0) & (frame_ids >= spacings), 1, 0).astype(jnp.int32)


def shard_levels(stream_key, dims, cuts, least, largest):
    loudness = 1.0
    for position, blocks in cuts:
        steps = jax.random.uniform(jax.random.fold_in(jax.random.fold_in(stream_key, 6), position), (blocks,), jnp.float32, least / len(cuts), largest / len(cuts))
        loudness = loudness * jnp.repeat(jnp.exp(steps), dims[position] // blocks).reshape((-1,) + (1,) * (len(dims) - 1 - position))
    return loudness


def gaussian(own_key, extent, width, bound, shards=(), dtype=jnp.bfloat16):
    level = shard_levels(own_key, extent, shards, -0.22, 0.18) if shards else 1.0
    result = jax.random.normal(own_key, extent, jnp.float32) * width * level
    return jnp.minimum(jnp.maximum(result, -bound), bound).astype(dtype)


def setup_inputs(seed: int = 0, part: int = 0) -> dict:
    arg_keys = jax.random.split(jax.random.key(seed), 9)
    part_keys = jax.random.split(jax.random.fold_in(arg_keys[8], part), 9)
    return {
        "queries": draw_queries(jax.random.fold_in(jax.random.fold_in(arg_keys[8], part), 71), part),
        "keys": draw_keys(jax.random.fold_in(jax.random.fold_in(arg_keys[8], part), 71), part),
        "values": gaussian(part_keys[2], (FRAMES, PATCH, D), 1.0, 6.0, ((0, 16),)),
        "grad_out": gaussian(part_keys[3], (FRAMES, PATCH, D), 1.0, 6.0, ((0, 16),)),
        "links": draw_links(jax.random.fold_in(jax.random.fold_in(arg_keys[8], part), 71), part),
        "w_query": gaussian(arg_keys[5], (D, D), D ** -0.5, 0.1875),
        "w_key": gaussian(arg_keys[6], (D, D), D ** -0.5, 0.1875),
        "w_value": gaussian(arg_keys[7], (D, D), D ** -0.5, 0.1875),
    }


def attention_core(query_f, grad_f, key_list, value_list, live_list, score_scale):
    live_mask = jnp.stack([m[:, None, None] for m in live_list])
    scores = jnp.stack([jnp.sum(query_f * k, axis=-1) for k in key_list]) * score_scale
    scores = jnp.where(live_mask > 0, scores, -1e30)
    highest = jnp.max(scores, axis=0)
    weights_raw = jnp.exp(scores - highest) * live_mask
    probability = weights_raw / jnp.sum(weights_raw, axis=0)
    grad_prob = jnp.stack([jnp.sum(grad_f * v, axis=-1) for v in value_list])
    inner_sum = jnp.sum(probability * grad_prob, axis=0)
    grad_score = probability * (grad_prob - inner_sum) * score_scale
    grad_query = jnp.zeros_like(query_f)
    grad_keys = []
    grad_values = []
    for i in range(len(key_list)):
        grad_query = grad_query + grad_score[i][..., None] * key_list[i]
        grad_keys.append(grad_score[i][..., None] * query_f)
        grad_values.append(probability[i][..., None] * grad_f)
    return grad_query, grad_keys, grad_values


def dot_transposed(left, weight):
    return lax.dot_general(left, weight, (((1,), (1,)), ((), ())), preferred_element_type=jnp.float32)


def reference(queries, keys, values, grad_out, links, w_query, w_key, w_value):
    frames, patches, model_width = queries.shape
    head_size = model_width // HEADS
    score_scale = head_size ** -0.5
    block_rows = 64 if patches % 64 == 0 else patches
    block_count = patches // block_rows

    def split_blocks(a):
        return a.reshape(frames, block_count, block_rows, model_width).transpose(1, 0, 2, 3)

    def spread_heads(a):
        return a.astype(jnp.float32).reshape(frames, block_rows, HEADS, head_size)

    def per_block(pieces):
        query_b, key_b, value_b, grad_b = pieces
        query_f = spread_heads(query_b)
        grad_f = spread_heads(grad_b)
        key_f = spread_heads(key_b)
        value_f = spread_heads(value_b)
        key_list = [key_f]
        value_list = [value_f]
        live_list = [jnp.ones((frames,), jnp.float32)]
        for j in range(NDIL):
            spacing = 2 ** j
            padding = jnp.zeros((spacing, block_rows, HEADS, head_size), jnp.float32)
            key_list.append(jnp.concatenate([padding, key_f[:frames - spacing]], axis=0))
            value_list.append(jnp.concatenate([padding, value_f[:frames - spacing]], axis=0))
            live_list.append((links[:, j] > 0).astype(jnp.float32))
        grad_query, grad_keys, grad_values = attention_core(query_f, grad_f, key_list, value_list, live_list, score_scale)
        key_total = grad_keys[0]
        value_total = grad_values[0]
        for j in range(NDIL):
            spacing = 2 ** j
            padding = jnp.zeros((spacing, block_rows, HEADS, head_size), jnp.float32)
            key_total = key_total + jnp.concatenate([grad_keys[j + 1][spacing:], padding], axis=0)
            value_total = value_total + jnp.concatenate([grad_values[j + 1][spacing:], padding], axis=0)
        shape_out = (frames, block_rows, model_width)
        return (grad_query.reshape(shape_out).astype(jnp.bfloat16),
                key_total.reshape(shape_out).astype(jnp.bfloat16),
                value_total.reshape(shape_out).astype(jnp.bfloat16))

    grad_query, grad_key, grad_value = lax.map(
        per_block, (split_blocks(queries), split_blocks(keys), split_blocks(values), split_blocks(grad_out)))

    def join_blocks(a):
        return a.transpose(1, 0, 2, 3).reshape(frames * patches, model_width)

    total = dot_transposed(join_blocks(grad_query), w_query)
    total = total + dot_transposed(join_blocks(grad_key), w_key)
    total = total + dot_transposed(join_blocks(grad_value), w_value)
    return total.reshape(frames, patches, model_width).astype(jnp.bfloat16)
```

```python
import functools

import jax
import jax.numpy as jnp
from jax import lax
from jax.experimental import pallas as pl
from jax.experimental.pallas import tpu as pltpu
from jax.sharding import PartitionSpec as P

HEADS = 16
NDIL = 4
LANES = 128
PIECE = 16
OFFSETS = (4, 2, 1, 4, -2, -1)
FULL, KEYS, BACK = 0, 1, 2
AT = (
    (0, 1, 2, 3, 4, 5, 6, 7),
    (3, 4, 5, 6, 7, 8, 9, 10),
    (0, 1, 3, 4, 5, 6, 7, 8),
)
SENT = (-3, -3, -3)
NEAR = (1, 1, 1)
MEET = (2, 2, 2)
PART_NEAR, PART_MID, COLLECT, FINISH = 3, 4, 6, 3


def dot_nn(left, right):
    return lax.dot_general(
        left, right, (((1,), (0,)), ((), ())), preferred_element_type=jnp.float32
    )


def kernel(n, chunks, rows, links_ref, q_ref, k_ref, v_ref, g_ref, wq_ref, wk_ref, wv_ref,
           out_ref, raw, full, keys, back, pair, solo, full_in, keys_in, back_in,
           part_out, part_in, prob_out, prob_in, dot_out, dot_in, kept, kept_mid, kept_near,
           base, query_part, prods, gather, spread, fold, stored, weights,
           own_sem, w_sem, send_sem, recv_sem, prob_send, prob_recv, dot_send, dot_recv,
           part_send, part_recv):
    width = q_ref.shape[-1]
    patches = q_ref.shape[1]
    head = width // HEADS
    scale = head ** (-0.5)
    half = rows // 2
    count = NDIL + 1
    span = HEADS * PIECE
    groups = width // span
    block = raw.shape[2]
    blocks = patches // block
    i = lax.axis_index("frame")
    f32, bf16 = jnp.float32, jnp.bfloat16

    own = (full, keys, back)
    slots = (full_in, keys_in, back_in)

    def place(kind):
        return (n - 1 - i, -1) if kind == BACK else (i, 1)

    def load(x, b):
        src = (q_ref, k_ref, v_ref, g_ref)[x]
        return pltpu.make_async_copy(
            src.at[0, pl.ds(b * block, block), :], raw.at[x, b], own_sem.at[x, b])

    def hop(kind, way, c):
        m, sign = place(kind)
        bit1, bit0 = (m // 2) % 2, m % 2
        mine, into = own[kind].at[c], slots[kind]
        src, slot, off, cond = (
            (mine, 2, 4, m + 4 < n),
            (mine, 1, 2, bit1 == 0),
            (mine, 0, 1, bit0 == 0),
            (into.at[2, c], 3, 4, jnp.logical_and(m >= 4, m + 4 < n)),
            (into.at[2, c], 1, -2, jnp.logical_and(m >= 4, bit1 == 1)),
            (into.at[1, c], 0, -1, jnp.logical_and(m >= 2, bit0 == 1)),
        )[way]
        copy = pltpu.make_async_remote_copy(
            src_ref=src, dst_ref=into.at[slot, c],
            send_sem=send_sem.at[kind, way, c], recv_sem=recv_sem.at[kind, slot, c],
            device_id={"frame": i + sign * off}, device_id_type=pl.DeviceIdType.MESH)
        return copy, cond

    def send(kind, way, c):
        copy, cond = hop(kind, way, c)

        @pl.when(cond)
        def _():
            copy.start()

    def arrive(kind, slot, c):
        m, sign = place(kind)

        @pl.when(m >= 2**slot)
        def _():
            pltpu.make_async_remote_copy(
                src_ref=own[kind].at[c], dst_ref=slots[kind].at[slot, c],
                send_sem=send_sem.at[kind, 0, c], recv_sem=recv_sem.at[kind, slot, c],
                device_id={"frame": i - sign * 2**slot},
                device_id_type=pl.DeviceIdType.MESH).wait_recv()

    def returns(slot):
        bit1, bit0 = (i // 2) % 2, i % 2
        if slot == 2:
            return [(0, -4, i >= 4)]
        if slot == 3:
            return [(3, -4, i >= 8)]
        if slot == 1:
            return [(1, -2, jnp.logical_and(i >= 2, bit1 == 1)),
                    (4, 2, jnp.logical_and(i >= 2, bit1 == 0))]
        return [(2, -1, bit0 == 1), (5, 1, jnp.logical_and(i >= 1, bit0 == 0))]

    def back_copy(slot, way, off, c):
        return pltpu.make_async_remote_copy(
            src_ref=part_out.at[slot, c], dst_ref=part_in.at[way, c],
            send_sem=part_send.at[slot, c], recv_sem=part_recv.at[way, c],
            device_id={"frame": i + off}, device_id_type=pl.DeviceIdType.MESH)

    def give_back(slot, c):
        for way, off, cond in returns(slot):
            @pl.when(cond)
            def _():
                back_copy(slot, way, off, c).start()

    def add_back(way, c, ref):
        cond = hop(FULL, way, c)[1]

        @pl.when(cond)
        def _():
            pltpu.make_async_remote_copy(
                src_ref=part_out.at[0, c], dst_ref=part_in.at[way, c],
                send_sem=part_send.at[0, c], recv_sem=part_recv.at[way, c],
                device_id={"frame": i + OFFSETS[way]},
                device_id_type=pl.DeviceIdType.MESH).wait_recv()
            ref[c] += part_in[way, c].astype(f32)

    def prob_copy(j, c):
        return pltpu.make_async_remote_copy(
            src_ref=prob_out.at[c, j + 1], dst_ref=prob_in.at[c, j],
            send_sem=prob_send.at[j, c], recv_sem=prob_recv.at[j, c],
            device_id={"frame": i - 2**j}, device_id_type=pl.DeviceIdType.MESH)

    def dot_copy(j, c):
        return pltpu.make_async_remote_copy(
            src_ref=dot_out.at[c, j], dst_ref=dot_in.at[c, j],
            send_sem=dot_send.at[j, c], recv_sem=dot_recv.at[j, c],
            device_id={"frame": i + 2**j}, device_id_type=pl.DeviceIdType.MESH)

    def direct(kind, c):
        for way in range(3):
            send(kind, way, c)

    barrier = pltpu.get_barrier_semaphore()
    peers = jnp.int32(0)
    for j in range(NDIL):
        for off in (2**j, -(2**j)):
            there = jnp.logical_and(i + off >= 0, i + off < n)
            peers = peers + there.astype(jnp.int32)

            @pl.when(there)
            def _():
                pl.semaphore_signal(barrier, inc=1, device_id={"frame": i + off},
                                    device_id_type=pl.DeviceIdType.MESH)

    upper = blocks // 2
    Q, K, V, G = range(4)
    order = ([(x, b) for b in range(upper, blocks) for x in (K, V)]
             + [(x, b) for b in range(upper) for x in (Q, G, K)]
             + [(x, b) for b in range(upper, blocks) for x in (Q, G)]
             + [(V, b) for b in range(upper)])
    for x, b in order:
        load(x, b).start()
    w_copies = [pltpu.make_async_copy(w, stored.at[x], w_sem.at[x])
                for x, w in enumerate((wq_ref, wk_ref, wv_ref))]
    for copy in w_copies:
        copy.start()

    def reorder(x, b):
        load(x, b).wait()
        turned = raw[x, b].T
        turned = jnp.concatenate(
            [turned[(h * groups + g) * PIECE:(h * groups + g + 1) * PIECE]
             for g in range(groups) for h in range(HEADS)], axis=0)
        value = turned.T
        per = block // rows
        for r in range(per):
            piece = value[r * rows:(r + 1) * rows]
            if b >= upper:
                c = (b - upper) * per + r
                if x in (K, V):
                    full[c, (K, V).index(x)] = piece
                else:
                    pair[c, (Q, G).index(x)] = piece
            else:
                c = b * per + r
                if x == K:
                    keys[c] = piece
                elif x == V:
                    solo[c] = piece
                else:
                    back[c, (Q, G).index(x)] = piece

    def shifted(kind, lag):
        return [t + lag for t in AT[kind]]

    per = block // rows
    done = []

    def first(kind, sources, start):
        early = [c for c, t in enumerate(shifted(kind, SENT[kind])) if t < 0]
        for b in range(start, start + -(-len(early) // per)):
            for x in sources:
                reorder(x, b)
                done.append((x, b))
        if kind == FULL:
            pl.semaphore_wait(barrier, peers)
        for c in early:
            direct(kind, c)

    first(FULL, (K, V), upper)
    first(BACK, (Q, G), 0)
    first(KEYS, (K,), 0)
    for x, b in order:
        if (x, b) not in done:
            reorder(x, b)

    feature = lax.broadcasted_iota(jnp.int32, (span, LANES), 0) // PIECE
    lane = lax.broadcasted_iota(jnp.int32, (span, LANES), 1) % HEADS
    gather[...] = jnp.where(feature == lane, 1.0, 0.0).astype(bf16)
    lane = lax.broadcasted_iota(jnp.int32, (LANES, span), 0)
    feature = lax.broadcasted_iota(jnp.int32, (LANES, span), 1) // PIECE
    for x in range(4):
        hit = jnp.logical_and(lane % HEADS == feature, lane // (2 * HEADS) == x)
        spread[:, x * span:(x + 1) * span] = jnp.where(hit, 1.0, 0.0).astype(bf16)
    lane = lax.broadcasted_iota(jnp.int32, (LANES, LANES), 0)
    feature = lax.broadcasted_iota(jnp.int32, (LANES, LANES), 1)
    for x in range(2):
        hit = jnp.logical_and(lane % HEADS == feature % HEADS, lane // (2 * HEADS) == 2 * x)
        fold[x] = jnp.where(hit, 1.0, 0.0).astype(bf16)

    for j in range(NDIL):
        @pl.when(i < 2**j)
        def _():
            for c in range(chunks):
                for part in range(2):
                    full_in[j, c, part] = jnp.zeros((rows, width), bf16)
                keys_in[j, c] = jnp.zeros((rows, width), bf16)
                dot_in[c, j] = jnp.zeros((half, LANES), bf16)

        @pl.when(i + 2**j >= n)
        def _():
            for c in range(chunks):
                for part in range(2):
                    back_in[j, c, part] = jnp.zeros((rows, width), bf16)
                prob_in[c, j] = jnp.zeros((half, LANES), bf16)
    lanes = lax.broadcasted_iota(jnp.int32, (rows, LANES), 1)
    group = (lanes // HEADS) % 4
    lower = lanes[:half] < LANES // 2

    for x in range(3):
        w_copies[x].wait()
        for b in range(width // LANES):
            turned = stored[x, :, b * LANES:(b + 1) * LANES].T
            for r in range(LANES // PIECE):
                at = b * (LANES // PIECE) + r
                to = (at % groups) * HEADS + at // groups
                weights[x, to * PIECE:(to + 1) * PIECE] = turned[r * PIECE:(r + 1) * PIECE]

    def pack(value):
        return jnp.where(lower, value[:half], value[half:]).astype(bf16)

    def split(value):
        high = value.astype(bf16)
        return high, (value - high.astype(f32)).astype(bf16)

    def dots(pairs):
        for x, (left, right) in enumerate(pairs):
            product = left.astype(f32) * right.astype(f32)
            total = product[:, :span]
            for g in range(1, groups):
                total += product[:, g * span:(g + 1) * span]
            high, low = split(total)
            prods[2 * x * rows:(2 * x + 1) * rows] = high
            prods[(2 * x + 1) * rows:(2 * x + 2) * rows] = low
        sums = dot_nn(prods[:2 * len(pairs) * rows], gather[...])
        return [sums[2 * x * rows:(2 * x + 1) * rows]
                + sums[(2 * x + 1) * rows:(2 * x + 2) * rows] for x in range(len(pairs))]

    def softmax_back(scores, grad_prob):
        live = [None] + [(links_ref[0, j] > 0).astype(f32) for j in range(NDIL)]
        scores = [s if j == 0 else jnp.where(live[j] > 0, s, -1e30)
                  for j, s in enumerate(scores)]
        highest = functools.reduce(jnp.maximum, scores)
        raw_prob = [jnp.exp(s - highest) for s in scores]
        raw_prob = [r if j == 0 else r * live[j] for j, r in enumerate(raw_prob)]
        total = functools.reduce(jnp.add, raw_prob)
        probability = [r / total for r in raw_prob]
        inner = functools.reduce(
            jnp.add, [p * g for p, g in zip(probability, grad_prob)])
        values = []
        for prob, grad in zip(probability, grad_prob):
            grad_score = prob * (grad - inner) * scale
            value = jnp.where(group < 2, grad_score, prob)
            high = value.astype(bf16).astype(f32)
            values.append(jnp.where(group % 2 == 0, high, value - high))
        return values

    def wide(factor):
        return jnp.concatenate([factor] * groups, axis=1)

    def weighted(factors, arrays):
        total = wide(factors[0]) * arrays[0].astype(f32)
        for factor, array in zip(factors[1:], arrays[1:]):
            total += wide(factor) * array.astype(f32)
        return total.astype(bf16)

    def relay_far(kind):
        def run(c):
            arrive(kind, 2, c)
            send(kind, 4, c)
            send(kind, 3, c)
        return run

    def relay_near(kind):
        def run(c):
            arrive(kind, 1, c)
            send(kind, 5, c)
        return run

    def attend(c):
        for slot in (0, 3):
            arrive(FULL, slot, c)
        query, grad = pair[c, 0], pair[c, 1]
        sources = [full.at[c]] + [full_in.at[j, c] for j in range(NDIL)]
        found = dots([(query, s[0]) for s in sources] + [(grad, s[1]) for s in sources])
        values = softmax_back([s * scale for s in found[:count]], found[count:])
        stack = jnp.concatenate([v.astype(bf16) for v in values], axis=0)
        factor = dot_nn(stack, spread[:, :2 * span])
        factors = [factor[j * rows:(j + 1) * rows] for j in range(count)]
        query_grad = weighted([f[:, :span] for f in factors], [s[0] for s in sources])
        query, grad = query.astype(f32), grad.astype(f32)
        key_parts = jnp.concatenate(
            [(wide(f[:, :span]) * query).astype(bf16) for f in factors], axis=0)
        value_parts = jnp.concatenate(
            [(wide(f[:, span:]) * grad).astype(bf16) for f in factors], axis=0)
        projected = dot_nn(key_parts, weights[1]) + dot_nn(value_parts, weights[2])

        def at(slot):
            return projected[(slot + 1) * rows:(slot + 2) * rows]

        for slot in (0, 3):
            part_out[slot, c] = at(slot).astype(bf16)
            give_back(slot, c)
        kept_near[c] = at(1)
        kept_mid[c] = at(2)
        base[c] = projected[:rows] + dot_nn(query_grad, weights[0])

    def part_near(c):
        add_back(5, c, kept_near)
        part_out[1, c] = kept_near[c].astype(bf16)
        give_back(1, c)

    def part_mid(c):
        add_back(3, c, kept_mid)
        add_back(4, c, kept_mid)
        part_out[2, c] = kept_mid[c].astype(bf16)
        give_back(2, c)

    def collect(c):
        for way in (2, 1, 0):
            add_back(way, c, base)
        out_ref[0, pl.ds(pl.multiple_of(patches // 2 + c * rows, rows), rows), :] = (
            base[c].astype(bf16))

    def meet(c):
        for slot in (0, 3):
            arrive(BACK, slot, c)
        found = dots([(back[c, 1], solo[c])]
                     + [(back_in[j, c, 1], solo[c]) for j in range(NDIL)])
        kept[c] = found[0]
        for j in range(NDIL):
            high = found[j + 1].astype(bf16).astype(f32)
            dot_out[c, j] = pack(jnp.where(group % 2 == 0, high, found[j + 1] - high))

            @pl.when(i + 2**j < n)
            def _():
                dot_copy(j, c).start()

    def soften(c):
        for slot in (0, 3):
            arrive(KEYS, slot, c)
        sources = [keys[c]] + [keys_in[j, c] for j in range(NDIL)]
        found = dots([(back[c, 0], s) for s in sources])
        for j in range(NDIL):
            @pl.when(i >= 2**j)
            def _():
                dot_copy(j, c).wait_recv()
        packed = dot_in[c].reshape(NDIL * half, LANES)
        folded = [dot_nn(packed, fold[x]) for x in range(2)]
        grad_prob = [kept[c]] + [
            jnp.concatenate([f[j * half:(j + 1) * half] for f in folded], axis=0)
            for j in range(NDIL)]
        values = softmax_back([s * scale for s in found], grad_prob)
        for j in range(count):
            prob_out[c, j] = pack(values[j])
        for j in range(NDIL):
            @pl.when(i >= 2**j)
            def _():
                prob_copy(j, c).start()
        stack = jnp.concatenate([v.astype(bf16) for v in values], axis=0)
        factor = dot_nn(stack, spread[:, :span])
        query_part[c] = weighted(
            [factor[j * rows:(j + 1) * rows] for j in range(count)], sources)

    def finish(c):
        result = dot_nn(query_part[c], weights[0])
        for j in range(NDIL):
            @pl.when(i + 2**j < n)
            def _():
                prob_copy(j, c).wait_recv()
        packed = jnp.concatenate(
            [prob_out[c, 0], prob_in[c].reshape(NDIL * half, LANES)], axis=0)
        factor = dot_nn(packed, spread[...])
        for part in range(2):
            halves = []
            for h in range(2):
                at = slice(h * half, (h + 1) * half)
                cols = slice((2 * h + part) * span, (2 * h + part + 1) * span)
                halves.append(weighted(
                    [factor[j * half:(j + 1) * half, cols] for j in range(count)],
                    [back[c, part, at]] + [back_in[j, c, part, at] for j in range(NDIL)]))
            result += dot_nn(jnp.concatenate(halves, axis=0), weights[1 + part])
        out_ref[0, pl.ds(pl.multiple_of(c * rows, rows), rows), :] = result.astype(bf16)

    kinds = (FULL, BACK, KEYS)
    plan = (
        [(shifted(kind, 0), relay_far(kind)) for kind in kinds]
        + [(shifted(kind, SENT[kind]), functools.partial(direct, kind)) for kind in kinds]
        + [(shifted(kind, NEAR[kind]), relay_near(kind)) for kind in kinds]
        + [
            (shifted(FULL, MEET[FULL]), attend),
            (shifted(FULL, PART_NEAR), part_near),
            (shifted(FULL, PART_MID), part_mid),
            (shifted(BACK, MEET[BACK]), meet),
            (shifted(KEYS, MEET[KEYS]), soften),
            (shifted(KEYS, FINISH), finish),
            (shifted(FULL, COLLECT), collect),
        ])
    steps = max(times[-1] for times, _ in plan) + 1

    def step(s, carry):
        for times, run in plan:
            late = [t for t in times if t >= 0]
            hit = functools.reduce(jnp.logical_or, [s == t for t in late])
            c = functools.reduce(
                jnp.add, [(s > t).astype(jnp.int32) for t in late]) + (len(times) - len(late))

            @pl.when(hit)
            def _():
                run(c)
        return carry

    lax.fori_loop(0, steps, step, 0)

    def drain(c, carry):
        for kind in range(3):
            for way in range(6):
                copy, cond = hop(kind, way, c)

                @pl.when(cond)
                def _():
                    copy.wait_send()
        for j in range(NDIL):
            for way, off, cond in returns(j):
                @pl.when(cond)
                def _():
                    back_copy(j, way, off, c).wait_send()

            @pl.when(i >= 2**j)
            def _():
                prob_copy(j, c).wait_send()

            @pl.when(i + 2**j < n)
            def _():
                dot_copy(j, c).wait_send()
        return carry

    lax.fori_loop(0, chunks, drain, 0)


def per_device(queries, keys, values, grad_out, links, w_query, w_key, w_value):
    frames, patches, width = queries.shape
    n = lax.axis_size("frame")
    rows = 32
    chunks = patches // (2 * rows)
    half = rows // 2
    block = LANES
    span = HEADS * PIECE
    hbm = pl.BlockSpec(memory_space=pl.ANY)
    f32, bf16 = jnp.float32, jnp.bfloat16
    dma = pltpu.SemaphoreType.DMA
    one = (rows, width)
    return pl.pallas_call(
        functools.partial(kernel, n, chunks, rows),
        out_shape=jax.ShapeDtypeStruct((frames, patches, width), bf16),
        in_specs=[pl.BlockSpec(memory_space=pltpu.SMEM)] + [hbm] * 7,
        out_specs=pl.BlockSpec(memory_space=pltpu.VMEM),
        scratch_shapes=[
            pltpu.VMEM((4, patches // block, block, width), bf16),
            pltpu.VMEM((chunks, 2) + one, bf16),
            pltpu.VMEM((chunks,) + one, bf16),
            pltpu.VMEM((chunks, 2) + one, bf16),
            pltpu.VMEM((chunks, 2) + one, bf16),
            pltpu.VMEM((chunks,) + one, bf16),
            pltpu.VMEM((NDIL, chunks, 2) + one, bf16),
            pltpu.VMEM((NDIL, chunks) + one, bf16),
            pltpu.VMEM((NDIL, chunks, 2) + one, bf16),
            pltpu.VMEM((NDIL, chunks) + one, bf16),
            pltpu.VMEM((6, chunks) + one, bf16),
            pltpu.VMEM((chunks, NDIL + 1, half, LANES), bf16),
            pltpu.VMEM((chunks, NDIL, half, LANES), bf16),
            pltpu.VMEM((chunks, NDIL, half, LANES), bf16),
            pltpu.VMEM((chunks, NDIL, half, LANES), bf16),
            pltpu.VMEM((chunks, rows, LANES), f32),
            pltpu.VMEM((chunks,) + one, f32),
            pltpu.VMEM((chunks,) + one, f32),
            pltpu.VMEM((chunks,) + one, f32),
            pltpu.VMEM((chunks,) + one, bf16),
            pltpu.VMEM((4 * (NDIL + 1) * rows, span), bf16),
            pltpu.VMEM((span, LANES), bf16),
            pltpu.VMEM((LANES, 4 * span), bf16),
            pltpu.VMEM((2, LANES, LANES), bf16),
            pltpu.VMEM((3, width, width), bf16),
            pltpu.VMEM((3, width, width), bf16),
            dma((4, patches // block)),
            dma((3,)),
            dma((3, 6, chunks)),
            dma((3, NDIL, chunks)),
            dma((NDIL, chunks)),
            dma((NDIL, chunks)),
            dma((NDIL, chunks)),
            dma((NDIL, chunks)),
            dma((NDIL, chunks)),
            dma((6, chunks)),
        ],
        compiler_params=pltpu.CompilerParams(
            collective_id=0, has_side_effects=True, vmem_limit_bytes=60 * 1024 * 1024),
    )(links, queries, keys, values, grad_out, w_query, w_key, w_value)


def solution(mesh):
    placed = (
        P(("dom", "frame"), None, None),
        P(("dom", "frame"), None, None),
        P(("dom", "frame"), None, None),
        P(("dom", "frame"), None, None),
        P(("dom", "frame"), None),
        P(),
        P(),
        P(),
    )
    return jax.shard_map(
        per_device,
        mesh=mesh,
        in_specs=placed,
        out_specs=P(("dom", "frame"), None, None),
        check_vma=False,
    )
```

```python
import functools

import jax
import jax.numpy as jnp
from jax import lax
from jax.experimental import pallas as pl
from jax.experimental.pallas import tpu as pltpu
from jax.sharding import PartitionSpec as P

HEADS = 16
BATCH = 4
NDIL = 4
LANES = 128
PIECE = 16
OFFSETS = (4, 2, 1, 4, -2, -1)
FULL, KEYS, BACK = 0, 1, 2
AT = (
    (1, 3, 5, 7, 8, 10, 11, 12),
    (6, 9, 12, 13, 15, 16, 17, 18),
    (0, 2, 3, 6, 7, 10, 11, 14),
)
SENT = (-6, -2, -7)
NEAR = (2, 3, 2)
MEET = (4, 4, 3)
PART_NEAR, PART_MID, COLLECT, FINISH = 4, 7, 10, 9
ORDER = (3, 9, 8, 0, 1, 13, 6, 14, 10, 12, 11, 5, 7, 2, 4, 15)


def dot_nn(left, right):
    return lax.dot_general(
        left, right, (((1,), (0,)), ((), ())), preferred_element_type=jnp.float32
    )


def kernel(n, chunks, rows, links_ref, q_ref, k_ref, v_ref, g_ref, wq_ref, wk_ref, wv_ref,
           out_ref, raw, full, keys, back, pair, solo, full_in, keys_in, back_in,
           part_out, part_in, prob_out, prob_in, dot_out, dot_in, kept, kept_mid, kept_near,
           base, grads, ready, prods, gather, spread, fold, stored, weights,
           own_sem, w_sem, send_sem, recv_sem, prob_send, prob_recv, dot_send, dot_recv,
           part_send, part_recv, out_sem):
    width = q_ref.shape[-1]
    patches = q_ref.shape[1]
    head = width // HEADS
    scale = head ** (-0.5)
    half = rows // 2
    count = NDIL + 1
    span = HEADS * PIECE
    groups = width // span
    block = raw.shape[2]
    blocks = patches // block
    batch = BATCH if chunks % BATCH == 0 else 1
    i = lax.axis_index("frame")
    f32, bf16 = jnp.float32, jnp.bfloat16

    own = (full, keys, back)
    slots = (full_in, keys_in, back_in)

    def place(kind):
        return (n - 1 - i, -1) if kind == BACK else (i, 1)

    def load(x, b):
        src = (q_ref, k_ref, v_ref, g_ref)[x]
        return pltpu.make_async_copy(
            src.at[0, pl.ds(b * block, block), :], raw.at[x, b], own_sem.at[x, b])

    def hop(kind, way, c):
        m, sign = place(kind)
        bit1, bit0 = (m // 2) % 2, m % 2
        mine, into = own[kind].at[c], slots[kind]
        src, slot, off, cond = (
            (mine, 2, 4, m + 4 < n),
            (mine, 1, 2, bit1 == 0),
            (mine, 0, 1, bit0 == 0),
            (into.at[2, c], 3, 4, jnp.logical_and(m >= 4, m + 4 < n)),
            (into.at[2, c], 1, -2, jnp.logical_and(m >= 4, bit1 == 1)),
            (into.at[1, c], 0, -1, jnp.logical_and(m >= 2, bit0 == 1)),
        )[way]
        copy = pltpu.make_async_remote_copy(
            src_ref=src, dst_ref=into.at[slot, c],
            send_sem=send_sem.at[kind, way, c], recv_sem=recv_sem.at[kind, slot, c],
            device_id={"frame": i + sign * off}, device_id_type=pl.DeviceIdType.MESH)
        return copy, cond

    def send(kind, way, c):
        copy, cond = hop(kind, way, c)

        @pl.when(cond)
        def _():
            copy.start()

    def arrive(kind, slot, c):
        m, sign = place(kind)

        @pl.when(m >= 2**slot)
        def _():
            pltpu.make_async_remote_copy(
                src_ref=own[kind].at[c], dst_ref=slots[kind].at[slot, c],
                send_sem=send_sem.at[kind, 0, c], recv_sem=recv_sem.at[kind, slot, c],
                device_id={"frame": i - sign * 2**slot},
                device_id_type=pl.DeviceIdType.MESH).wait_recv()

    def returns(slot):
        bit1, bit0 = (i // 2) % 2, i % 2
        if slot == 2:
            return [(0, -4, i >= 4)]
        if slot == 3:
            return [(3, -4, i >= 8)]
        if slot == 1:
            return [(1, -2, jnp.logical_and(i >= 2, bit1 == 1)),
                    (4, 2, jnp.logical_and(i >= 2, bit1 == 0))]
        return [(2, -1, bit0 == 1), (5, 1, jnp.logical_and(i >= 1, bit0 == 0))]

    def back_copy(slot, way, off, c):
        return pltpu.make_async_remote_copy(
            src_ref=part_out.at[slot, c], dst_ref=part_in.at[way, c],
            send_sem=part_send.at[slot, c], recv_sem=part_recv.at[way, c],
            device_id={"frame": i + off}, device_id_type=pl.DeviceIdType.MESH)

    def give_back(slot, c):
        for way, off, cond in returns(slot):
            @pl.when(cond)
            def _():
                back_copy(slot, way, off, c).start()

    def add_back(way, c, ref):
        cond = hop(FULL, way, c)[1]

        @pl.when(cond)
        def _():
            pltpu.make_async_remote_copy(
                src_ref=part_out.at[0, c], dst_ref=part_in.at[way, c],
                send_sem=part_send.at[0, c], recv_sem=part_recv.at[way, c],
                device_id={"frame": i + OFFSETS[way]},
                device_id_type=pl.DeviceIdType.MESH).wait_recv()
            ref[c] += part_in[way, c].astype(f32)

    def prob_copy(j, c):
        return pltpu.make_async_remote_copy(
            src_ref=prob_out.at[c, j + 1], dst_ref=prob_in.at[c, j],
            send_sem=prob_send.at[j, c], recv_sem=prob_recv.at[j, c],
            device_id={"frame": i - 2**j}, device_id_type=pl.DeviceIdType.MESH)

    def dot_copy(j, c):
        return pltpu.make_async_remote_copy(
            src_ref=dot_out.at[c, j], dst_ref=dot_in.at[c, j],
            send_sem=dot_send.at[j, c], recv_sem=dot_recv.at[j, c],
            device_id={"frame": i + 2**j}, device_id_type=pl.DeviceIdType.MESH)

    def direct(kind, c):
        for way in range(3):
            send(kind, way, c)

    barrier = pltpu.get_barrier_semaphore()
    peers = jnp.int32(0)
    for j in range(NDIL):
        for off in (2**j, -(2**j)):
            there = jnp.logical_and(i + off >= 0, i + off < n)
            peers = peers + there.astype(jnp.int32)

            @pl.when(there)
            def _():
                pl.semaphore_signal(barrier, inc=1, device_id={"frame": i + off},
                                    device_id_type=pl.DeviceIdType.MESH)

    upper = blocks // 2
    Q, K, V, G = range(4)
    order = ([(x, b) for b in range(upper, blocks) for x in (K, V)]
             + [(x, b) for b in range(upper) for x in (Q, G, K)]
             + [(x, b) for b in range(upper, blocks) for x in (Q, G)]
             + [(V, b) for b in range(upper)])
    for x, b in order:
        load(x, b).start()
    w_copies = [pltpu.make_async_copy(w, stored.at[x], w_sem.at[x])
                for x, w in enumerate((wq_ref, wk_ref, wv_ref))]
    for copy in w_copies:
        copy.start()

    def reorder(x, b):
        load(x, b).wait()
        turned = raw[x, b].T
        turned = jnp.concatenate(
            [turned[(h * groups + g) * PIECE:(h * groups + g + 1) * PIECE]
             for g in range(groups) for h in range(HEADS)], axis=0)
        value = turned.T
        per = block // rows
        for r in range(per):
            piece = value[r * rows:(r + 1) * rows]
            if b >= upper:
                c = (b - upper) * per + r
                if x in (K, V):
                    full[c, (K, V).index(x)] = piece
                else:
                    pair[c, (Q, G).index(x)] = piece
            else:
                c = b * per + r
                if x == K:
                    keys[c] = piece
                elif x == V:
                    solo[c] = piece
                else:
                    back[c, (Q, G).index(x)] = piece

    def shifted(kind, lag):
        return [t + lag for t in AT[kind]]

    per = block // rows
    done = []

    def first(kind, sources, start):
        early = [c for c, t in enumerate(shifted(kind, SENT[kind])) if t < 0]
        for b in range(start, start + -(-len(early) // per)):
            for x in sources:
                reorder(x, b)
                done.append((x, b))
        if kind == FULL:
            pl.semaphore_wait(barrier, peers)
        for c in early:
            direct(kind, c)

    first(FULL, (K, V), upper)
    first(BACK, (Q, G), 0)
    first(KEYS, (K,), 0)
    for x, b in order:
        if (x, b) not in done:
            reorder(x, b)

    feature = lax.broadcasted_iota(jnp.int32, (span, LANES), 0) // PIECE
    lane = lax.broadcasted_iota(jnp.int32, (span, LANES), 1) % HEADS
    gather[...] = jnp.where(feature == lane, 1.0, 0.0).astype(bf16)
    lane = lax.broadcasted_iota(jnp.int32, (LANES, span), 0)
    feature = lax.broadcasted_iota(jnp.int32, (LANES, span), 1) // PIECE
    for x in range(4):
        hit = jnp.logical_and(lane % HEADS == feature, lane // (2 * HEADS) == x)
        spread[:, x * span:(x + 1) * span] = jnp.where(hit, 1.0, 0.0).astype(bf16)
    lane = lax.broadcasted_iota(jnp.int32, (LANES, LANES), 0)
    feature = lax.broadcasted_iota(jnp.int32, (LANES, LANES), 1)
    for x in range(2):
        hit = jnp.logical_and(lane % HEADS == feature % HEADS, lane // (2 * HEADS) == 2 * x)
        fold[x] = jnp.where(hit, 1.0, 0.0).astype(bf16)

    for j in range(NDIL):
        @pl.when(i < 2**j)
        def _():
            for c in range(chunks):
                for part in range(2):
                    full_in[j, c, part] = jnp.zeros((rows, width), bf16)
                keys_in[j, c] = jnp.zeros((rows, width), bf16)
                dot_in[c, j] = jnp.zeros((half, LANES), bf16)

        @pl.when(i + 2**j >= n)
        def _():
            for c in range(chunks):
                for part in range(2):
                    back_in[j, c, part] = jnp.zeros((rows, width), bf16)
                prob_in[c, j] = jnp.zeros((half, LANES), bf16)
    lanes = lax.broadcasted_iota(jnp.int32, (rows, LANES), 1)
    group = (lanes // HEADS) % 4
    lower = lanes[:half] < LANES // 2

    for x in range(3):
        w_copies[x].wait()
        for b in range(width // LANES):
            turned = stored[x, :, b * LANES:(b + 1) * LANES].T
            for r in range(LANES // PIECE):
                at = b * (LANES // PIECE) + r
                to = (at % groups) * HEADS + at // groups
                weights[x, to * PIECE:(to + 1) * PIECE] = turned[r * PIECE:(r + 1) * PIECE]

    def pack(value):
        return jnp.where(lower, value[:half], value[half:]).astype(bf16)

    def split(value):
        high = value.astype(bf16)
        return high, (value - high.astype(f32)).astype(bf16)

    def dots(pairs):
        for x, (left, right) in enumerate(pairs):
            product = left.astype(f32) * right.astype(f32)
            total = product[:, :span]
            for g in range(1, groups):
                total += product[:, g * span:(g + 1) * span]
            high, low = split(total)
            prods[2 * x * rows:(2 * x + 1) * rows] = high
            prods[(2 * x + 1) * rows:(2 * x + 2) * rows] = low
        sums = dot_nn(prods[:2 * len(pairs) * rows], gather[...])
        return [sums[2 * x * rows:(2 * x + 1) * rows]
                + sums[(2 * x + 1) * rows:(2 * x + 2) * rows] for x in range(len(pairs))]

    def softmax_back(scores, grad_prob):
        live = [None] + [(links_ref[0, j] > 0).astype(f32) for j in range(NDIL)]
        scores = [s if j == 0 else jnp.where(live[j] > 0, s, -1e30)
                  for j, s in enumerate(scores)]
        highest = functools.reduce(jnp.maximum, scores)
        raw_prob = [jnp.exp(s - highest) for s in scores]
        raw_prob = [r if j == 0 else r * live[j] for j, r in enumerate(raw_prob)]
        total = functools.reduce(jnp.add, raw_prob)
        probability = [r / total for r in raw_prob]
        inner = functools.reduce(
            jnp.add, [p * g for p, g in zip(probability, grad_prob)])
        values = []
        for prob, grad in zip(probability, grad_prob):
            grad_score = prob * (grad - inner) * scale
            value = jnp.where(group < 2, grad_score, prob)
            high = value.astype(bf16).astype(f32)
            values.append(jnp.where(group % 2 == 0, high, value - high))
        return values

    def wide(factor):
        return jnp.concatenate([factor] * groups, axis=1)

    def weighted(factors, arrays):
        total = wide(factors[0]) * arrays[0].astype(f32)
        for factor, array in zip(factors[1:], arrays[1:]):
            total += wide(factor) * array.astype(f32)
        return total.astype(bf16)

    def relay_far(kind):
        def run(c):
            arrive(kind, 2, c)
            send(kind, 4, c)
            send(kind, 3, c)
        return run

    def relay_near(kind):
        def run(c):
            arrive(kind, 1, c)
            send(kind, 5, c)
        return run

    def attend(c):
        for slot in (0, 3):
            arrive(FULL, slot, c)
        query, grad = pair[c, 0], pair[c, 1]
        sources = [full.at[c]] + [full_in.at[j, c] for j in range(NDIL)]
        found = dots([(query, s[0]) for s in sources] + [(grad, s[1]) for s in sources])
        values = softmax_back([s * scale for s in found[:count]], found[count:])
        stack = jnp.concatenate([v.astype(bf16) for v in values], axis=0)
        factor = dot_nn(stack, spread[:, :2 * span])
        factors = [factor[j * rows:(j + 1) * rows] for j in range(count)]
        query_grad = weighted([f[:, :span] for f in factors], [s[0] for s in sources])
        query, grad = query.astype(f32), grad.astype(f32)
        key_parts = jnp.concatenate(
            [(wide(f[:, :span]) * query).astype(bf16) for f in factors], axis=0)
        value_parts = jnp.concatenate(
            [(wide(f[:, span:]) * grad).astype(bf16) for f in factors], axis=0)
        projected = dot_nn(key_parts, weights[1]) + dot_nn(value_parts, weights[2])

        def at(slot):
            return projected[(slot + 1) * rows:(slot + 2) * rows]

        for slot in (0, 3):
            part_out[slot, c] = at(slot).astype(bf16)
            give_back(slot, c)
        kept_near[c] = at(1)
        kept_mid[c] = at(2)
        base[c] = projected[:rows]
        grads[3, c] = query_grad

    def part_near(c):
        add_back(5, c, kept_near)
        part_out[1, c] = kept_near[c].astype(bf16)
        give_back(1, c)

    def part_mid(c):
        add_back(3, c, kept_mid)
        add_back(4, c, kept_mid)
        part_out[2, c] = kept_mid[c].astype(bf16)
        give_back(2, c)

    def batched(c, run):
        @pl.when(c % batch == batch - 1)
        def _():
            run(c + 1 - batch)

    def rows_of(array):
        return array.reshape(batch * rows, width)

    def write(side, c):
        at = pl.multiple_of(side * (patches // 2) + c * rows, rows)
        return pltpu.make_async_copy(
            ready.at[pl.ds(at, batch * rows), :],
            out_ref.at[0, pl.ds(at, batch * rows), :], out_sem.at[side, c // batch])

    def put(side, c, value):
        at = pl.multiple_of(side * (patches // 2) + c * rows, rows)
        ready[pl.ds(at, batch * rows), :] = value.astype(bf16)
        write(side, c).start()

    def collect(c):
        for way in (2, 1, 0):
            add_back(way, c, base)

        def last(first):
            put(1, first, rows_of(base[pl.ds(first, batch)])
                + dot_nn(rows_of(grads[3, pl.ds(first, batch)]), weights[0]))
        batched(c, last)

    def meet(c):
        for slot in (0, 3):
            arrive(BACK, slot, c)
        found = dots([(back[c, 1], solo[c])]
                     + [(back_in[j, c, 1], solo[c]) for j in range(NDIL)])
        kept[c] = found[0]
        for j in range(NDIL):
            high = found[j + 1].astype(bf16).astype(f32)
            dot_out[c, j] = pack(jnp.where(group % 2 == 0, high, found[j + 1] - high))

            @pl.when(i + 2**j < n)
            def _():
                dot_copy(j, c).start()

    def soften(c):
        for slot in (0, 3):
            arrive(KEYS, slot, c)
        sources = [keys[c]] + [keys_in[j, c] for j in range(NDIL)]
        found = dots([(back[c, 0], s) for s in sources])
        for j in range(NDIL):
            @pl.when(i >= 2**j)
            def _():
                dot_copy(j, c).wait_recv()
        packed = dot_in[c].reshape(NDIL * half, LANES)
        folded = [dot_nn(packed, fold[x]) for x in range(2)]
        grad_prob = [kept[c]] + [
            jnp.concatenate([f[j * half:(j + 1) * half] for f in folded], axis=0)
            for j in range(NDIL)]
        values = softmax_back([s * scale for s in found], grad_prob)
        for j in range(count):
            prob_out[c, j] = pack(values[j])
        for j in range(NDIL):
            @pl.when(i >= 2**j)
            def _():
                prob_copy(j, c).start()
        stack = jnp.concatenate([v.astype(bf16) for v in values], axis=0)
        factor = dot_nn(stack, spread[:, :span])
        grads[0, c] = weighted(
            [factor[j * rows:(j + 1) * rows] for j in range(count)], sources)

    def finish(c):
        for j in range(NDIL):
            @pl.when(i + 2**j < n)
            def _():
                prob_copy(j, c).wait_recv()
        packed = jnp.concatenate(
            [prob_out[c, 0], prob_in[c].reshape(NDIL * half, LANES)], axis=0)
        factor = dot_nn(packed, spread[...])
        for part in range(2):
            halves = []
            for h in range(2):
                at = slice(h * half, (h + 1) * half)
                cols = slice((2 * h + part) * span, (2 * h + part + 1) * span)
                halves.append(weighted(
                    [factor[j * half:(j + 1) * half, cols] for j in range(count)],
                    [back[c, part, at]] + [back_in[j, c, part, at] for j in range(NDIL)]))
            grads[1 + part, c] = jnp.concatenate(halves, axis=0)

        def last(first):
            put(0, first, functools.reduce(jnp.add, [
                dot_nn(rows_of(grads[x, pl.ds(first, batch)]), weights[x])
                for x in range(3)]))
        batched(c, last)

    kinds = (FULL, BACK, KEYS)
    plan = (
        [(shifted(kind, 0), relay_far(kind)) for kind in kinds]
        + [(shifted(kind, SENT[kind]), functools.partial(direct, kind)) for kind in kinds]
        + [(shifted(kind, NEAR[kind]), relay_near(kind)) for kind in kinds]
        + [
            (shifted(FULL, MEET[FULL]), attend),
            (shifted(FULL, PART_NEAR), part_near),
            (shifted(FULL, PART_MID), part_mid),
            (shifted(BACK, MEET[BACK]), meet),
            (shifted(KEYS, MEET[KEYS]), soften),
            (shifted(KEYS, FINISH), finish),
            (shifted(FULL, COLLECT), collect),
        ])
    plan = [plan[x] for x in ORDER]
    steps = max(times[-1] for times, _ in plan) + 1

    def step(s, carry):
        for times, run in plan:
            late = [t for t in times if t >= 0]
            hit = functools.reduce(jnp.logical_or, [s == t for t in late])
            c = functools.reduce(
                jnp.add, [(s > t).astype(jnp.int32) for t in late]) + (len(times) - len(late))

            @pl.when(hit)
            def _():
                run(c)
        return carry

    lax.fori_loop(0, steps, step, 0)

    def drain(c, carry):
        for kind in range(3):
            for way in range(6):
                copy, cond = hop(kind, way, c)

                @pl.when(cond)
                def _():
                    copy.wait_send()
        for j in range(NDIL):
            for way, off, cond in returns(j):
                @pl.when(cond)
                def _():
                    back_copy(j, way, off, c).wait_send()

            @pl.when(i >= 2**j)
            def _():
                prob_copy(j, c).wait_send()

            @pl.when(i + 2**j < n)
            def _():
                dot_copy(j, c).wait_send()
        return carry

    lax.fori_loop(0, chunks, drain, 0)
    for side in range(2):
        for c in range(0, chunks, batch):
            write(side, c).wait()


def per_device(queries, keys, values, grad_out, links, w_query, w_key, w_value):
    frames, patches, width = queries.shape
    n = lax.axis_size("frame")
    rows = 32
    chunks = patches // (2 * rows)
    half = rows // 2
    block = LANES
    span = HEADS * PIECE
    hbm = pl.BlockSpec(memory_space=pl.ANY)
    f32, bf16 = jnp.float32, jnp.bfloat16
    dma = pltpu.SemaphoreType.DMA
    one = (rows, width)
    return pl.pallas_call(
        functools.partial(kernel, n, chunks, rows),
        out_shape=jax.ShapeDtypeStruct((frames, patches, width), bf16),
        in_specs=[pl.BlockSpec(memory_space=pltpu.SMEM)] + [hbm] * 7,
        out_specs=hbm,
        scratch_shapes=[
            pltpu.VMEM((4, patches // block, block, width), bf16),
            pltpu.VMEM((chunks, 2) + one, bf16),
            pltpu.VMEM((chunks,) + one, bf16),
            pltpu.VMEM((chunks, 2) + one, bf16),
            pltpu.VMEM((chunks, 2) + one, bf16),
            pltpu.VMEM((chunks,) + one, bf16),
            pltpu.VMEM((NDIL, chunks, 2) + one, bf16),
            pltpu.VMEM((NDIL, chunks) + one, bf16),
            pltpu.VMEM((NDIL, chunks, 2) + one, bf16),
            pltpu.VMEM((NDIL, chunks) + one, bf16),
            pltpu.VMEM((6, chunks) + one, bf16),
            pltpu.VMEM((chunks, NDIL + 1, half, LANES), bf16),
            pltpu.VMEM((chunks, NDIL, half, LANES), bf16),
            pltpu.VMEM((chunks, NDIL, half, LANES), bf16),
            pltpu.VMEM((chunks, NDIL, half, LANES), bf16),
            pltpu.VMEM((chunks, rows, LANES), f32),
            pltpu.VMEM((chunks,) + one, f32),
            pltpu.VMEM((chunks,) + one, f32),
            pltpu.VMEM((chunks,) + one, f32),
            pltpu.VMEM((4, chunks) + one, bf16),
            pltpu.VMEM((patches, width), bf16),
            pltpu.VMEM((4 * (NDIL + 1) * rows, span), bf16),
            pltpu.VMEM((span, LANES), bf16),
            pltpu.VMEM((LANES, 4 * span), bf16),
            pltpu.VMEM((2, LANES, LANES), bf16),
            pltpu.VMEM((3, width, width), bf16),
            pltpu.VMEM((3, width, width), bf16),
            dma((4, patches // block)),
            dma((3,)),
            dma((3, 6, chunks)),
            dma((3, NDIL, chunks)),
            dma((NDIL, chunks)),
            dma((NDIL, chunks)),
            dma((NDIL, chunks)),
            dma((NDIL, chunks)),
            dma((NDIL, chunks)),
            dma((6, chunks)),
            dma((2, chunks)),
        ],
        compiler_params=pltpu.CompilerParams(
            collective_id=0, has_side_effects=True, vmem_limit_bytes=60 * 1024 * 1024),
    )(links, queries, keys, values, grad_out, w_query, w_key, w_value)


def solution(mesh):
    placed = (
        P(("dom", "frame"), None, None),
        P(("dom", "frame"), None, None),
        P(("dom", "frame"), None, None),
        P(("dom", "frame"), None, None),
        P(("dom", "frame"), None),
        P(),
        P(),
        P(),
    )
    return jax.shard_map(
        per_device,
        mesh=mesh,
        in_specs=placed,
        out_specs=P(("dom", "frame"), None, None),
        check_vma=False,
    )
```

```python
import functools

import jax
import jax.numpy as jnp
from jax import lax
from jax.experimental import pallas as pl
from jax.experimental.pallas import tpu as pltpu
from jax.sharding import PartitionSpec as P

HEADS = 16
BATCH = 4
NDIL = 4
LANES = 128
PIECE = 16
OFFSETS = (4, 2, 1, 4, -2, -1)
FULL, KEYS, BACK = 0, 1, 2
ALL = slice(None)
AT = (
    (1, 3, 5, 7, 8, 10, 11, 12),
    (6, 9, 12, 13, 15, 16, 17, 18),
    (0, 2, 3, 6, 7, 10, 11, 14),
)
SENT = (-6, -2, -7)
NEAR = (2, 3, 2)
MEET = (4, 4, 3)
PART_NEAR, PART_MID, COLLECT, FINISH = 4, 7, 10, 9
ORDER = (3, 9, 8, 0, 1, 13, 6, 14, 10, 12, 11, 5, 7, 2, 4, 15)


def dot_nn(left, right):
    return lax.dot_general(
        left, right, (((1,), (0,)), ((), ())), preferred_element_type=jnp.float32
    )


def kernel(n, chunks, rows, links_ref, q_ref, k_ref, v_ref, g_ref, wq_ref, wk_ref, wv_ref,
           out_ref, raw, full, keys, back, pair, solo, full_in, keys_in, back_in,
           part_out, part_in, prob_out, prob_in, dot_out, dot_in, kept, kept_mid, kept_near,
           base, total, grads, ready, prods, gather, spread, fold, stored, weights,
           own_sem, w_sem, send_sem, recv_sem, prob_send, prob_recv, dot_send, dot_recv,
           part_send, part_recv, out_sem):
    width = q_ref.shape[-1]
    patches = q_ref.shape[1]
    head = width // HEADS
    scale = head ** (-0.5)
    half = rows // 2
    count = NDIL + 1
    span = HEADS * PIECE
    groups = width // span
    block = raw.shape[2]
    blocks = patches // block
    batch = BATCH if chunks % BATCH == 0 else 1
    i = lax.axis_index("frame")
    f32, bf16 = jnp.float32, jnp.bfloat16

    own = (full, keys, back)
    slots = (full_in, keys_in, back_in)

    def place(kind):
        return (n - 1 - i, -1) if kind == BACK else (i, 1)

    def load(x, b):
        src = (q_ref, k_ref, v_ref, g_ref)[x]
        return pltpu.make_async_copy(
            src.at[0, pl.ds(b * block, block), :], raw.at[x, b], own_sem.at[x, b])

    def hop(kind, way, c):
        m, sign = place(kind)
        bit1, bit0 = (m // 2) % 2, m % 2
        mine, into = own[kind].at[c], slots[kind]
        src, slot, off, cond = (
            (mine, 2, 4, m + 4 < n),
            (mine, 1, 2, bit1 == 0),
            (mine, 0, 1, bit0 == 0),
            (into.at[2, c], 3, 4, jnp.logical_and(m >= 4, m + 4 < n)),
            (into.at[2, c], 1, -2, jnp.logical_and(m >= 4, bit1 == 1)),
            (into.at[1, c], 0, -1, jnp.logical_and(m >= 2, bit0 == 1)),
        )[way]
        copy = pltpu.make_async_remote_copy(
            src_ref=src, dst_ref=into.at[slot, c],
            send_sem=send_sem.at[kind, way], recv_sem=recv_sem.at[kind, slot, 0 if c is ALL else c],
            device_id={"frame": i + sign * off}, device_id_type=pl.DeviceIdType.MESH)
        return copy, cond

    def send(kind, way, c):
        copy, cond = hop(kind, way, c)

        @pl.when(cond)
        def _():
            copy.start()

    def arrive(kind, slot, c):
        m, sign = place(kind)

        @pl.when(m >= 2**slot)
        def _():
            pltpu.make_async_remote_copy(
                src_ref=own[kind].at[c], dst_ref=slots[kind].at[slot, c],
                send_sem=send_sem.at[kind, 0], recv_sem=recv_sem.at[kind, slot, c],
                device_id={"frame": i - sign * 2**slot},
                device_id_type=pl.DeviceIdType.MESH).wait_recv()

    def returns(slot):
        bit1, bit0 = (i // 2) % 2, i % 2
        if slot == 2:
            return [(0, -4, i >= 4)]
        if slot == 3:
            return [(3, -4, i >= 8)]
        if slot == 1:
            return [(1, -2, jnp.logical_and(i >= 2, bit1 == 1)),
                    (4, 2, jnp.logical_and(i >= 2, bit1 == 0))]
        return [(2, -1, bit0 == 1), (5, 1, jnp.logical_and(i >= 1, bit0 == 0))]

    def back_copy(slot, way, off, c):
        return pltpu.make_async_remote_copy(
            src_ref=part_out.at[slot, c], dst_ref=part_in.at[way, c],
            send_sem=part_send.at[slot], recv_sem=part_recv.at[way, 0 if c is ALL else c],
            device_id={"frame": i + off}, device_id_type=pl.DeviceIdType.MESH)

    def give_back(slot, c):
        for way, off, cond in returns(slot):
            @pl.when(cond)
            def _():
                back_copy(slot, way, off, c).start()

    def add_back(way, c, ref):
        cond = hop(FULL, way, c)[1]

        @pl.when(cond)
        def _():
            pltpu.make_async_remote_copy(
                src_ref=part_out.at[0, c], dst_ref=part_in.at[way, c],
                send_sem=part_send.at[0], recv_sem=part_recv.at[way, c],
                device_id={"frame": i + OFFSETS[way]},
                device_id_type=pl.DeviceIdType.MESH).wait_recv()
            ref[c] += part_in[way, c].astype(f32)

    def prob_copy(j, c):
        return pltpu.make_async_remote_copy(
            src_ref=prob_out.at[c, j + 1], dst_ref=prob_in.at[c, j],
            send_sem=prob_send.at[j], recv_sem=prob_recv.at[j, 0 if c is ALL else c],
            device_id={"frame": i - 2**j}, device_id_type=pl.DeviceIdType.MESH)

    def dot_copy(j, c):
        return pltpu.make_async_remote_copy(
            src_ref=dot_out.at[c, j], dst_ref=dot_in.at[c, j],
            send_sem=dot_send.at[j], recv_sem=dot_recv.at[j, 0 if c is ALL else c],
            device_id={"frame": i + 2**j}, device_id_type=pl.DeviceIdType.MESH)

    def direct(kind, c):
        for way in range(3):
            send(kind, way, c)

    upper = blocks // 2
    Q, K, V, G = range(4)
    order = ([(x, b) for b in range(upper, blocks) for x in (K, V)]
             + [(x, b) for b in range(upper) for x in (Q, G, K)]
             + [(x, b) for b in range(upper, blocks) for x in (Q, G)]
             + [(V, b) for b in range(upper)])
    head_loads = [(K, upper), (V, upper), (Q, 0), (G, 0)]
    for x, b in head_loads:
        load(x, b).start()

    barrier = pltpu.get_barrier_semaphore()
    peers = jnp.int32(0)
    for j in range(NDIL):
        for off in (2**j, -(2**j)):
            there = jnp.logical_and(i + off >= 0, i + off < n)
            peers = peers + there.astype(jnp.int32)

            @pl.when(there)
            def _():
                pl.semaphore_signal(barrier, inc=1, device_id={"frame": i + off},
                                    device_id_type=pl.DeviceIdType.MESH)

    w_copies = [pltpu.make_async_copy(w, stored.at[x], w_sem.at[x])
                for x, w in enumerate((wq_ref, wk_ref, wv_ref))]

    def reorder(x, b):
        load(x, b).wait()
        turned = raw[x, b].T
        turned = jnp.concatenate(
            [turned[(h * groups + g) * PIECE:(h * groups + g + 1) * PIECE]
             for g in range(groups) for h in range(HEADS)], axis=0)
        value = turned.T
        per = block // rows
        for r in range(per):
            piece = value[r * rows:(r + 1) * rows]
            if b >= upper:
                c = (b - upper) * per + r
                if x in (K, V):
                    full[c, (K, V).index(x)] = piece
                else:
                    pair[c, (Q, G).index(x)] = piece
            else:
                c = b * per + r
                if x == K:
                    keys[c] = piece
                elif x == V:
                    solo[c] = piece
                else:
                    back[c, (Q, G).index(x)] = piece

    def shifted(kind, lag):
        return [t + lag for t in AT[kind]]

    per = block // rows
    done = []

    def first(kind, sources, start):
        early = [c for c, t in enumerate(shifted(kind, SENT[kind])) if t < 0]
        for b in range(start, start + -(-len(early) // per)):
            for x in sources:
                reorder(x, b)
                done.append((x, b))
        if kind == FULL:
            for x, b in order:
                if (x, b) not in head_loads:
                    load(x, b).start()
            for copy in w_copies:
                copy.start()
            pl.semaphore_wait(barrier, peers)
        for c in early:
            direct(kind, c)

    first(FULL, (K, V), upper)
    first(BACK, (Q, G), 0)
    first(KEYS, (K,), 0)
    for x, b in order:
        if (x, b) not in done:
            reorder(x, b)

    feature = lax.broadcasted_iota(jnp.int32, (span, LANES), 0) // PIECE
    lane = lax.broadcasted_iota(jnp.int32, (span, LANES), 1) % HEADS
    gather[...] = jnp.where(feature == lane, 1.0, 0.0).astype(bf16)
    lane = lax.broadcasted_iota(jnp.int32, (LANES, span), 0)
    feature = lax.broadcasted_iota(jnp.int32, (LANES, span), 1) // PIECE
    for x in range(4):
        hit = jnp.logical_and(lane % HEADS == feature, lane // (2 * HEADS) == x)
        spread[:, x * span:(x + 1) * span] = jnp.where(hit, 1.0, 0.0).astype(bf16)
    lane = lax.broadcasted_iota(jnp.int32, (LANES, LANES), 0)
    feature = lax.broadcasted_iota(jnp.int32, (LANES, LANES), 1)
    for x in range(2):
        hit = jnp.logical_and(lane % HEADS == feature % HEADS, lane // (2 * HEADS) == 2 * x)
        fold[x] = jnp.where(hit, 1.0, 0.0).astype(bf16)

    for j in range(NDIL):
        @pl.when(i < 2**j)
        def _():
            for c in range(chunks):
                for part in range(2):
                    full_in[j, c, part] = jnp.zeros((rows, width), bf16)
                keys_in[j, c] = jnp.zeros((rows, width), bf16)
                dot_in[c, j] = jnp.zeros((half, LANES), bf16)

        @pl.when(i + 2**j >= n)
        def _():
            for c in range(chunks):
                for part in range(2):
                    back_in[j, c, part] = jnp.zeros((rows, width), bf16)
                prob_in[c, j] = jnp.zeros((half, LANES), bf16)
    lanes = lax.broadcasted_iota(jnp.int32, (rows, LANES), 1)
    group = (lanes // HEADS) % 4
    lower = lanes[:half] < LANES // 2

    for x in range(3):
        w_copies[x].wait()
        for b in range(width // LANES):
            turned = stored[x, :, b * LANES:(b + 1) * LANES].T
            for r in range(LANES // PIECE):
                at = b * (LANES // PIECE) + r
                to = (at % groups) * HEADS + at // groups
                weights[x, to * PIECE:(to + 1) * PIECE] = turned[r * PIECE:(r + 1) * PIECE]

    def pack(value):
        return jnp.where(lower, value[:half], value[half:]).astype(bf16)

    def split(value):
        high = value.astype(bf16)
        return high, (value - high.astype(f32)).astype(bf16)

    def dots(pairs):
        for x, (left, right) in enumerate(pairs):
            product = left.astype(f32) * right.astype(f32)
            total = product[:, :span]
            for g in range(1, groups):
                total += product[:, g * span:(g + 1) * span]
            high, low = split(total)
            prods[2 * x * rows:(2 * x + 1) * rows] = high
            prods[(2 * x + 1) * rows:(2 * x + 2) * rows] = low
        sums = dot_nn(prods[:2 * len(pairs) * rows], gather[...])
        return [sums[2 * x * rows:(2 * x + 1) * rows]
                + sums[(2 * x + 1) * rows:(2 * x + 2) * rows] for x in range(len(pairs))]

    def softmax_back(scores, grad_prob):
        live = [None] + [(links_ref[0, j] > 0).astype(f32) for j in range(NDIL)]
        scores = [s if j == 0 else jnp.where(live[j] > 0, s, -1e30)
                  for j, s in enumerate(scores)]
        highest = functools.reduce(jnp.maximum, scores)
        raw_prob = [jnp.exp(s - highest) for s in scores]
        raw_prob = [r if j == 0 else r * live[j] for j, r in enumerate(raw_prob)]
        total = functools.reduce(jnp.add, raw_prob)
        probability = [r / total for r in raw_prob]
        inner = functools.reduce(
            jnp.add, [p * g for p, g in zip(probability, grad_prob)])
        values = []
        for prob, grad in zip(probability, grad_prob):
            grad_score = prob * (grad - inner) * scale
            value = jnp.where(group < 2, grad_score, prob)
            high = value.astype(bf16).astype(f32)
            values.append(jnp.where(group % 2 == 0, high, value - high))
        return values

    def wide(factor):
        return jnp.concatenate([factor] * groups, axis=1)

    def weighted(factors, arrays):
        total = wide(factors[0]) * arrays[0].astype(f32)
        for factor, array in zip(factors[1:], arrays[1:]):
            total += wide(factor) * array.astype(f32)
        return total.astype(bf16)

    def relay_far(kind):
        def run(c):
            arrive(kind, 2, c)
            send(kind, 4, c)
            send(kind, 3, c)
        return run

    def relay_near(kind):
        def run(c):
            arrive(kind, 1, c)
            send(kind, 5, c)
        return run

    def attend(c):
        for slot in (0, 3):
            arrive(FULL, slot, c)
        query, grad = pair[c, 0], pair[c, 1]
        sources = [full.at[c]] + [full_in.at[j, c] for j in range(NDIL)]
        found = dots([(query, s[0]) for s in sources] + [(grad, s[1]) for s in sources])
        values = softmax_back([s * scale for s in found[:count]], found[count:])
        stack = jnp.concatenate([v.astype(bf16) for v in values], axis=0)
        factor = dot_nn(stack, spread[:, :2 * span])
        factors = [factor[j * rows:(j + 1) * rows] for j in range(count)]
        query_grad = weighted([f[:, :span] for f in factors], [s[0] for s in sources])
        query, grad = query.astype(f32), grad.astype(f32)
        key_parts = jnp.concatenate(
            [(wide(f[:, :span]) * query).astype(bf16) for f in factors], axis=0)
        value_parts = jnp.concatenate(
            [(wide(f[:, span:]) * grad).astype(bf16) for f in factors], axis=0)
        projected = dot_nn(key_parts, weights[1]) + dot_nn(value_parts, weights[2])

        def at(slot):
            return projected[(slot + 1) * rows:(slot + 2) * rows]

        for slot in (0, 3):
            part_out[slot, c] = at(slot).astype(bf16)
            give_back(slot, c)
        kept_near[c] = at(1)
        kept_mid[c] = at(2)
        base[c] = projected[:rows]
        grads[3, c] = query_grad

        def last(first):
            part = dot_nn(rows_of(grads[3, pl.ds(first, batch)]), weights[0])
            base[pl.ds(first, batch)] += part.reshape(batch, rows, width)
        batched(c, last)

    def part_near(c):
        add_back(5, c, kept_near)
        part_out[1, c] = kept_near[c].astype(bf16)
        give_back(1, c)

    def part_mid(c):
        add_back(3, c, kept_mid)
        add_back(4, c, kept_mid)
        part_out[2, c] = kept_mid[c].astype(bf16)
        give_back(2, c)

    def batched(c, run):
        @pl.when(c % batch == batch - 1)
        def _():
            run(c + 1 - batch)

    def rows_of(array):
        return array.reshape(batch * rows, width)

    def write(side, c):
        at = pl.multiple_of(side * (patches // 2) + c * rows, rows)
        return pltpu.make_async_copy(
            ready.at[pl.ds(at, batch * rows), :],
            out_ref.at[0, pl.ds(at, batch * rows), :], out_sem.at[side, c // batch])

    def put(side, c, value):
        at = pl.multiple_of(side * (patches // 2) + c * rows, rows)
        ready[pl.ds(at, batch * rows), :] = value.astype(bf16)
        write(side, c).start()

    def collect(c):
        for way in (2, 1, 0):
            add_back(way, c, base)

        def last(first):
            put(1, first, rows_of(base[pl.ds(first, batch)]))
        batched(c, last)

    def meet(c):
        for slot in (0, 3):
            arrive(BACK, slot, c)
        found = dots([(back[c, 1], solo[c])]
                     + [(back_in[j, c, 1], solo[c]) for j in range(NDIL)])
        kept[c] = found[0]
        for j in range(NDIL):
            high = found[j + 1].astype(bf16).astype(f32)
            dot_out[c, j] = pack(jnp.where(group % 2 == 0, high, found[j + 1] - high))

            @pl.when(i + 2**j < n)
            def _():
                dot_copy(j, c).start()

    def soften(c):
        for slot in (0, 3):
            arrive(KEYS, slot, c)
        sources = [keys[c]] + [keys_in[j, c] for j in range(NDIL)]
        found = dots([(back[c, 0], s) for s in sources])
        for j in range(NDIL):
            @pl.when(i >= 2**j)
            def _():
                dot_copy(j, c).wait_recv()
        packed = dot_in[c].reshape(NDIL * half, LANES)
        folded = [dot_nn(packed, fold[x]) for x in range(2)]
        grad_prob = [kept[c]] + [
            jnp.concatenate([f[j * half:(j + 1) * half] for f in folded], axis=0)
            for j in range(NDIL)]
        values = softmax_back([s * scale for s in found], grad_prob)
        for j in range(count):
            prob_out[c, j] = pack(values[j])
        for j in range(NDIL):
            @pl.when(i >= 2**j)
            def _():
                prob_copy(j, c).start()
        stack = jnp.concatenate([v.astype(bf16) for v in values], axis=0)
        factor = dot_nn(stack, spread[:, :span])
        grads[0, c] = weighted(
            [factor[j * rows:(j + 1) * rows] for j in range(count)], sources)

        def last(first):
            part = dot_nn(rows_of(grads[0, pl.ds(first, batch)]), weights[0])
            total[pl.ds(first, batch)] = part.reshape(batch, rows, width)
        batched(c, last)

    def finish(c):
        for j in range(NDIL):
            @pl.when(i + 2**j < n)
            def _():
                prob_copy(j, c).wait_recv()
        packed = jnp.concatenate(
            [prob_out[c, 0], prob_in[c].reshape(NDIL * half, LANES)], axis=0)
        factor = dot_nn(packed, spread[...])
        for part in range(2):
            halves = []
            for h in range(2):
                at = slice(h * half, (h + 1) * half)
                cols = slice((2 * h + part) * span, (2 * h + part + 1) * span)
                halves.append(weighted(
                    [factor[j * half:(j + 1) * half, cols] for j in range(count)],
                    [back[c, part, at]] + [back_in[j, c, part, at] for j in range(NDIL)]))
            grads[1 + part, c] = jnp.concatenate(halves, axis=0)

        def last(first):
            put(0, first, functools.reduce(jnp.add, [
                dot_nn(rows_of(grads[x, pl.ds(first, batch)]), weights[x])
                for x in (1, 2)], rows_of(total[pl.ds(first, batch)])))
        batched(c, last)

    kinds = (FULL, BACK, KEYS)
    plan = (
        [(shifted(kind, 0), relay_far(kind)) for kind in kinds]
        + [(shifted(kind, SENT[kind]), functools.partial(direct, kind)) for kind in kinds]
        + [(shifted(kind, NEAR[kind]), relay_near(kind)) for kind in kinds]
        + [
            (shifted(FULL, MEET[FULL]), attend),
            (shifted(FULL, PART_NEAR), part_near),
            (shifted(FULL, PART_MID), part_mid),
            (shifted(BACK, MEET[BACK]), meet),
            (shifted(KEYS, MEET[KEYS]), soften),
            (shifted(KEYS, FINISH), finish),
            (shifted(FULL, COLLECT), collect),
        ])
    plan = [plan[x] for x in ORDER]
    steps = max(times[-1] for times, _ in plan) + 1

    def step(s, carry):
        for times, run in plan:
            late = [t for t in times if t >= 0]
            hit = functools.reduce(jnp.logical_or, [s == t for t in late])
            c = functools.reduce(
                jnp.add, [(s > t).astype(jnp.int32) for t in late]) + (len(times) - len(late))

            @pl.when(hit)
            def _():
                run(c)
        return carry

    lax.fori_loop(0, steps, step, 0)

    for kind in range(3):
        for way in range(6):
            copy, cond = hop(kind, way, ALL)

            @pl.when(cond)
            def _():
                copy.wait_send()
    for j in range(NDIL):
        for way, off, cond in returns(j):
            @pl.when(cond)
            def _():
                back_copy(j, way, off, ALL).wait_send()

        @pl.when(i >= 2**j)
        def _():
            prob_copy(j, ALL).wait_send()

        @pl.when(i + 2**j < n)
        def _():
            dot_copy(j, ALL).wait_send()
    for side in range(2):
        for c in range(0, chunks, batch):
            write(side, c).wait()


def per_device(queries, keys, values, grad_out, links, w_query, w_key, w_value):
    frames, patches, width = queries.shape
    n = lax.axis_size("frame")
    rows = 32
    chunks = patches // (2 * rows)
    half = rows // 2
    block = LANES
    span = HEADS * PIECE
    hbm = pl.BlockSpec(memory_space=pl.ANY)
    f32, bf16 = jnp.float32, jnp.bfloat16
    dma = pltpu.SemaphoreType.DMA
    one = (rows, width)
    return pl.pallas_call(
        functools.partial(kernel, n, chunks, rows),
        out_shape=jax.ShapeDtypeStruct((frames, patches, width), bf16),
        in_specs=[pl.BlockSpec(memory_space=pltpu.SMEM)] + [hbm] * 7,
        out_specs=hbm,
        scratch_shapes=[
            pltpu.VMEM((4, patches // block, block, width), bf16),
            pltpu.VMEM((chunks, 2) + one, bf16),
            pltpu.VMEM((chunks,) + one, bf16),
            pltpu.VMEM((chunks, 2) + one, bf16),
            pltpu.VMEM((chunks, 2) + one, bf16),
            pltpu.VMEM((chunks,) + one, bf16),
            pltpu.VMEM((NDIL, chunks, 2) + one, bf16),
            pltpu.VMEM((NDIL, chunks) + one, bf16),
            pltpu.VMEM((NDIL, chunks, 2) + one, bf16),
            pltpu.VMEM((NDIL, chunks) + one, bf16),
            pltpu.VMEM((6, chunks) + one, bf16),
            pltpu.VMEM((chunks, NDIL + 1, half, LANES), bf16),
            pltpu.VMEM((chunks, NDIL, half, LANES), bf16),
            pltpu.VMEM((chunks, NDIL, half, LANES), bf16),
            pltpu.VMEM((chunks, NDIL, half, LANES), bf16),
            pltpu.VMEM((chunks, rows, LANES), f32),
            pltpu.VMEM((chunks,) + one, f32),
            pltpu.VMEM((chunks,) + one, f32),
            pltpu.VMEM((chunks,) + one, f32),
            pltpu.VMEM((chunks,) + one, f32),
            pltpu.VMEM((4, chunks) + one, bf16),
            pltpu.VMEM((patches, width), bf16),
            pltpu.VMEM((4 * (NDIL + 1) * rows, span), bf16),
            pltpu.VMEM((span, LANES), bf16),
            pltpu.VMEM((LANES, 4 * span), bf16),
            pltpu.VMEM((2, LANES, LANES), bf16),
            pltpu.VMEM((3, width, width), bf16),
            pltpu.VMEM((3, width, width), bf16),
            dma((4, patches // block)),
            dma((3,)),
            dma((3, 6)),
            dma((3, NDIL, chunks)),
            dma((NDIL,)),
            dma((NDIL, chunks)),
            dma((NDIL,)),
            dma((NDIL, chunks)),
            dma((NDIL,)),
            dma((6, chunks)),
            dma((2, chunks)),
        ],
        compiler_params=pltpu.CompilerParams(
            collective_id=0, has_side_effects=True, vmem_limit_bytes=60 * 1024 * 1024),
    )(links, queries, keys, values, grad_out, w_query, w_key, w_value)


def solution(mesh):
    placed = (
        P(("dom", "frame"), None, None),
        P(("dom", "frame"), None, None),
        P(("dom", "frame"), None, None),
        P(("dom", "frame"), None, None),
        P(("dom", "frame"), None),
        P(),
        P(),
        P(),
    )
    return jax.shard_map(
        per_device,
        mesh=mesh,
        in_specs=placed,
        out_specs=P(("dom", "frame"), None, None),
        check_vma=False,
    )
```

```python
import functools

import jax
import jax.numpy as jnp
from jax import lax
from jax.experimental import pallas as pl
from jax.experimental.pallas import tpu as pltpu
from jax.sharding import PartitionSpec as P

HEADS = 16
BATCH = 4
NDIL = 4
LANES = 128
PIECE = 16
OFFSETS = (4, 2, 1, 4, -2, -1)
FULL, KEYS, BACK = 0, 1, 2
ALL = slice(None)
AT = (
    (1, 3, 5, 7, 8, 10, 11, 12),
    (6, 9, 12, 13, 15, 16, 17, 18),
    (0, 2, 3, 6, 7, 10, 11, 14),
)
SENT = (-6, -3, -7)
NEAR = (2, 3, 2)
MEET = (4, 4, 3)
PART_NEAR, PART_MID, COLLECT, FINISH = 4, 7, 10, 9
ORDER = (3, 9, 8, 0, 1, 13, 6, 14, 10, 12, 11, 5, 7, 2, 4, 15)


def dot_nn(left, right):
    return lax.dot_general(
        left, right, (((1,), (0,)), ((), ())), preferred_element_type=jnp.float32
    )


def kernel(n, chunks, rows, links_ref, q_ref, k_ref, v_ref, g_ref, wq_ref, wk_ref, wv_ref,
           out_ref, raw, full, keys, back, pair, solo, full_in, keys_in, back_in,
           part_out, part_in, prob_out, prob_in, dot_out, dot_in, kept, kept_mid, kept_near,
           base, total, grads, ready, prods, gather, spread, fold, stored, weights,
           own_sem, w_sem, send_sem, recv_sem, prob_send, prob_recv, dot_send, dot_recv,
           part_send, part_recv, out_sem):
    width = q_ref.shape[-1]
    patches = q_ref.shape[1]
    head = width // HEADS
    scale = head ** (-0.5)
    half = rows // 2
    count = NDIL + 1
    span = HEADS * PIECE
    groups = width // span
    block = raw.shape[2]
    blocks = patches // block
    batch = BATCH if chunks % BATCH == 0 else 1
    i = lax.axis_index("frame")
    f32, bf16 = jnp.float32, jnp.bfloat16

    own = (full, keys, back)
    slots = (full_in, keys_in, back_in)

    def place(kind):
        return (n - 1 - i, -1) if kind == BACK else (i, 1)

    def load(x, b):
        src = (q_ref, k_ref, v_ref, g_ref)[x]
        return pltpu.make_async_copy(
            src.at[0, pl.ds(b * block, block), :], raw.at[x, b], own_sem.at[x, b])

    def hop(kind, way, c):
        m, sign = place(kind)
        bit1, bit0 = (m // 2) % 2, m % 2
        mine, into = own[kind].at[c], slots[kind]
        src, slot, off, cond = (
            (mine, 2, 4, m + 4 < n),
            (mine, 1, 2, bit1 == 0),
            (mine, 0, 1, bit0 == 0),
            (into.at[2, c], 3, 4, jnp.logical_and(m >= 4, m + 4 < n)),
            (into.at[2, c], 1, -2, jnp.logical_and(m >= 4, bit1 == 1)),
            (into.at[1, c], 0, -1, jnp.logical_and(m >= 2, bit0 == 1)),
        )[way]
        copy = pltpu.make_async_remote_copy(
            src_ref=src, dst_ref=into.at[slot, c],
            send_sem=send_sem.at[kind, way], recv_sem=recv_sem.at[kind, slot, 0 if c is ALL else c],
            device_id={"frame": i + sign * off}, device_id_type=pl.DeviceIdType.MESH)
        return copy, cond

    def send(kind, way, c):
        copy, cond = hop(kind, way, c)

        @pl.when(cond)
        def _():
            copy.start()

    def arrive(kind, slot, c):
        m, sign = place(kind)

        @pl.when(m >= 2**slot)
        def _():
            pltpu.make_async_remote_copy(
                src_ref=own[kind].at[c], dst_ref=slots[kind].at[slot, c],
                send_sem=send_sem.at[kind, 0], recv_sem=recv_sem.at[kind, slot, c],
                device_id={"frame": i - sign * 2**slot},
                device_id_type=pl.DeviceIdType.MESH).wait_recv()

    def returns(slot):
        bit1, bit0 = (i // 2) % 2, i % 2
        if slot == 2:
            return [(0, -4, i >= 4)]
        if slot == 3:
            return [(3, -4, i >= 8)]
        if slot == 1:
            return [(1, -2, jnp.logical_and(i >= 2, bit1 == 1)),
                    (4, 2, jnp.logical_and(i >= 2, bit1 == 0))]
        return [(2, -1, bit0 == 1), (5, 1, jnp.logical_and(i >= 1, bit0 == 0))]

    def back_copy(slot, way, off, c):
        return pltpu.make_async_remote_copy(
            src_ref=part_out.at[slot, c], dst_ref=part_in.at[way, c],
            send_sem=part_send.at[slot], recv_sem=part_recv.at[way, 0 if c is ALL else c],
            device_id={"frame": i + off}, device_id_type=pl.DeviceIdType.MESH)

    def give_back(slot, c):
        for way, off, cond in returns(slot):
            @pl.when(cond)
            def _():
                back_copy(slot, way, off, c).start()

    def add_back(way, c, ref):
        cond = hop(FULL, way, c)[1]

        @pl.when(cond)
        def _():
            pltpu.make_async_remote_copy(
                src_ref=part_out.at[0, c], dst_ref=part_in.at[way, c],
                send_sem=part_send.at[0], recv_sem=part_recv.at[way, c],
                device_id={"frame": i + OFFSETS[way]},
                device_id_type=pl.DeviceIdType.MESH).wait_recv()
            ref[c] += part_in[way, c].astype(f32)

    def prob_copy(j, c):
        return pltpu.make_async_remote_copy(
            src_ref=prob_out.at[c, j + 1], dst_ref=prob_in.at[c, j],
            send_sem=prob_send.at[j], recv_sem=prob_recv.at[j, 0 if c is ALL else c],
            device_id={"frame": i - 2**j}, device_id_type=pl.DeviceIdType.MESH)

    def dot_copy(j, c):
        return pltpu.make_async_remote_copy(
            src_ref=dot_out.at[c, j], dst_ref=dot_in.at[c, j],
            send_sem=dot_send.at[j], recv_sem=dot_recv.at[j, 0 if c is ALL else c],
            device_id={"frame": i + 2**j}, device_id_type=pl.DeviceIdType.MESH)

    def direct(kind, c):
        for way in range(3):
            send(kind, way, c)

    upper = blocks // 2
    Q, K, V, G = range(4)
    order = ([(x, b) for b in range(upper, blocks) for x in (K, V)]
             + [(x, b) for b in range(upper) for x in (Q, G, K)]
             + [(x, b) for b in range(upper, blocks) for x in (Q, G)]
             + [(V, b) for b in range(upper)])
    head_loads = [(K, upper), (V, upper), (Q, 0), (G, 0)]
    for x, b in head_loads:
        load(x, b).start()

    barrier = pltpu.get_barrier_semaphore()
    peers = jnp.int32(0)
    for j in range(NDIL):
        for off in (2**j, -(2**j)):
            there = jnp.logical_and(i + off >= 0, i + off < n)
            peers = peers + there.astype(jnp.int32)

            @pl.when(there)
            def _():
                pl.semaphore_signal(barrier, inc=1, device_id={"frame": i + off},
                                    device_id_type=pl.DeviceIdType.MESH)

    w_copies = [pltpu.make_async_copy(w, stored.at[x], w_sem.at[x])
                for x, w in enumerate((wq_ref, wk_ref, wv_ref))]

    def reorder(x, b):
        load(x, b).wait()
        turned = raw[x, b].T
        turned = jnp.concatenate(
            [turned[(h * groups + g) * PIECE:(h * groups + g + 1) * PIECE]
             for g in range(groups) for h in range(HEADS)], axis=0)
        value = turned.T
        per = block // rows
        for r in range(per):
            piece = value[r * rows:(r + 1) * rows]
            if b >= upper:
                c = (b - upper) * per + r
                if x in (K, V):
                    full[c, (K, V).index(x)] = piece
                else:
                    pair[c, (Q, G).index(x)] = piece
            else:
                c = b * per + r
                if x == K:
                    keys[c] = piece
                elif x == V:
                    solo[c] = piece
                else:
                    back[c, (Q, G).index(x)] = piece

    def shifted(kind, lag):
        return [t + lag for t in AT[kind]]

    per = block // rows
    done = []

    def first(kind, sources, start):
        early = [c for c, t in enumerate(shifted(kind, SENT[kind])) if t < 0]
        for b in range(start, start + -(-len(early) // per)):
            for x in sources:
                reorder(x, b)
                done.append((x, b))
        if kind == FULL:
            for x, b in order:
                if (x, b) not in head_loads:
                    load(x, b).start()
            for copy in w_copies:
                copy.start()
            pl.semaphore_wait(barrier, peers)
        for c in early:
            direct(kind, c)

    first(FULL, (K, V), upper)
    first(BACK, (Q, G), 0)
    first(KEYS, (K,), 0)
    for x, b in order:
        if (x, b) not in done:
            reorder(x, b)

    feature = lax.broadcasted_iota(jnp.int32, (span, LANES), 0) // PIECE
    lane = lax.broadcasted_iota(jnp.int32, (span, LANES), 1) % HEADS
    gather[...] = jnp.where(feature == lane, 1.0, 0.0).astype(bf16)
    lane = lax.broadcasted_iota(jnp.int32, (LANES, span), 0)
    feature = lax.broadcasted_iota(jnp.int32, (LANES, span), 1) // PIECE
    for x in range(4):
        hit = jnp.logical_and(lane % HEADS == feature, lane // (2 * HEADS) == x)
        spread[:, x * span:(x + 1) * span] = jnp.where(hit, 1.0, 0.0).astype(bf16)
    lane = lax.broadcasted_iota(jnp.int32, (LANES, LANES), 0)
    feature = lax.broadcasted_iota(jnp.int32, (LANES, LANES), 1)
    for x in range(2):
        hit = jnp.logical_and(lane % HEADS == feature % HEADS, lane // (2 * HEADS) == 2 * x)
        fold[x] = jnp.where(hit, 1.0, 0.0).astype(bf16)

    for j in range(NDIL):
        @pl.when(i < 2**j)
        def _():
            for c in range(chunks):
                for part in range(2):
                    full_in[j, c, part] = jnp.zeros((rows, width), bf16)
                keys_in[j, c] = jnp.zeros((rows, width), bf16)
                dot_in[c, j] = jnp.zeros((half, LANES), bf16)

        @pl.when(i + 2**j >= n)
        def _():
            for c in range(chunks):
                for part in range(2):
                    back_in[j, c, part] = jnp.zeros((rows, width), bf16)
                prob_in[c, j] = jnp.zeros((half, LANES), bf16)
    lanes = lax.broadcasted_iota(jnp.int32, (rows, LANES), 1)
    group = (lanes // HEADS) % 4
    lower = lanes[:half] < LANES // 2

    for x in range(3):
        w_copies[x].wait()
        for b in range(width // LANES):
            turned = stored[x, :, b * LANES:(b + 1) * LANES].T
            for r in range(LANES // PIECE):
                at = b * (LANES // PIECE) + r
                to = (at % groups) * HEADS + at // groups
                weights[x, to * PIECE:(to + 1) * PIECE] = turned[r * PIECE:(r + 1) * PIECE]

    def pack(value):
        return jnp.where(lower, value[:half], value[half:]).astype(bf16)

    def split(value):
        high = value.astype(bf16)
        return high, (value - high.astype(f32)).astype(bf16)

    def dots(pairs):
        for x, (left, right) in enumerate(pairs):
            product = left.astype(f32) * right.astype(f32)
            total = product[:, :span]
            for g in range(1, groups):
                total += product[:, g * span:(g + 1) * span]
            high, low = split(total)
            prods[2 * x * rows:(2 * x + 1) * rows] = high
            prods[(2 * x + 1) * rows:(2 * x + 2) * rows] = low
        sums = dot_nn(prods[:2 * len(pairs) * rows], gather[...])
        return [sums[2 * x * rows:(2 * x + 1) * rows]
                + sums[(2 * x + 1) * rows:(2 * x + 2) * rows] for x in range(len(pairs))]

    def softmax_back(scores, grad_prob):
        live = [None] + [(links_ref[0, j] > 0).astype(f32) for j in range(NDIL)]
        scores = [s if j == 0 else jnp.where(live[j] > 0, s, -1e30)
                  for j, s in enumerate(scores)]
        highest = functools.reduce(jnp.maximum, scores)
        raw_prob = [jnp.exp(s - highest) for s in scores]
        raw_prob = [r if j == 0 else r * live[j] for j, r in enumerate(raw_prob)]
        total = functools.reduce(jnp.add, raw_prob)
        probability = [r / total for r in raw_prob]
        inner = functools.reduce(
            jnp.add, [p * g for p, g in zip(probability, grad_prob)])
        values = []
        for prob, grad in zip(probability, grad_prob):
            grad_score = prob * (grad - inner) * scale
            value = jnp.where(group < 2, grad_score, prob)
            high = value.astype(bf16).astype(f32)
            values.append(jnp.where(group % 2 == 0, high, value - high))
        return values

    def wide(factor):
        return jnp.concatenate([factor] * groups, axis=1)

    def weighted(factors, arrays):
        total = wide(factors[0]) * arrays[0].astype(f32)
        for factor, array in zip(factors[1:], arrays[1:]):
            total += wide(factor) * array.astype(f32)
        return total.astype(bf16)

    def relay_far(kind):
        def run(c):
            arrive(kind, 2, c)
            send(kind, 4, c)
            send(kind, 3, c)
        return run

    def relay_near(kind):
        def run(c):
            arrive(kind, 1, c)
            send(kind, 5, c)
        return run

    def attend(c):
        for slot in (0, 3):
            arrive(FULL, slot, c)
        query, grad = pair[c, 0], pair[c, 1]
        sources = [full.at[c]] + [full_in.at[j, c] for j in range(NDIL)]
        found = dots([(query, s[0]) for s in sources] + [(grad, s[1]) for s in sources])
        values = softmax_back([s * scale for s in found[:count]], found[count:])
        stack = jnp.concatenate([v.astype(bf16) for v in values], axis=0)
        factor = dot_nn(stack, spread[:, :2 * span])
        factors = [factor[j * rows:(j + 1) * rows] for j in range(count)]
        query_grad = weighted([f[:, :span] for f in factors], [s[0] for s in sources])
        query, grad = query.astype(f32), grad.astype(f32)
        key_parts = jnp.concatenate(
            [(wide(f[:, :span]) * query).astype(bf16) for f in factors], axis=0)
        value_parts = jnp.concatenate(
            [(wide(f[:, span:]) * grad).astype(bf16) for f in factors], axis=0)
        projected = dot_nn(key_parts, weights[1]) + dot_nn(value_parts, weights[2])

        def at(slot):
            return projected[(slot + 1) * rows:(slot + 2) * rows]

        for slot in (0, 3):
            part_out[slot, c] = at(slot).astype(bf16)
            give_back(slot, c)
        kept_near[c] = at(1)
        kept_mid[c] = at(2)
        base[c] = projected[:rows]
        grads[3, c] = query_grad

        def last(first):
            part = dot_nn(rows_of(grads[3, pl.ds(first, batch)]), weights[0])
            base[pl.ds(first, batch)] += part.reshape(batch, rows, width)
        batched(c, last)

    def part_near(c):
        add_back(5, c, kept_near)
        part_out[1, c] = kept_near[c].astype(bf16)
        give_back(1, c)

    def part_mid(c):
        add_back(3, c, kept_mid)
        add_back(4, c, kept_mid)
        part_out[2, c] = kept_mid[c].astype(bf16)
        give_back(2, c)

    def batched(c, run):
        @pl.when(c % batch == batch - 1)
        def _():
            run(c + 1 - batch)

    def rows_of(array):
        return array.reshape(batch * rows, width)

    def write(side, c):
        at = pl.multiple_of(side * (patches // 2) + c * rows, rows)
        return pltpu.make_async_copy(
            ready.at[pl.ds(at, batch * rows), :],
            out_ref.at[0, pl.ds(at, batch * rows), :], out_sem.at[side, c // batch])

    def put(side, c, value):
        at = pl.multiple_of(side * (patches // 2) + c * rows, rows)
        ready[pl.ds(at, batch * rows), :] = value.astype(bf16)
        write(side, c).start()

    def collect(c):
        for way in (2, 1, 0):
            add_back(way, c, base)

        def last(first):
            put(1, first, rows_of(base[pl.ds(first, batch)]))
        batched(c, last)

    def meet(c):
        for slot in (0, 3):
            arrive(BACK, slot, c)
        found = dots([(back[c, 1], solo[c])]
                     + [(back_in[j, c, 1], solo[c]) for j in range(NDIL)])
        kept[c] = found[0]
        for j in range(NDIL):
            high = found[j + 1].astype(bf16).astype(f32)
            dot_out[c, j] = pack(jnp.where(group % 2 == 0, high, found[j + 1] - high))

            @pl.when(i + 2**j < n)
            def _():
                dot_copy(j, c).start()

    def soften(c):
        for slot in (0, 3):
            arrive(KEYS, slot, c)
        sources = [keys[c]] + [keys_in[j, c] for j in range(NDIL)]
        found = dots([(back[c, 0], s) for s in sources])
        for j in range(NDIL):
            @pl.when(i >= 2**j)
            def _():
                dot_copy(j, c).wait_recv()
        packed = dot_in[c].reshape(NDIL * half, LANES)
        folded = [dot_nn(packed, fold[x]) for x in range(2)]
        grad_prob = [kept[c]] + [
            jnp.concatenate([f[j * half:(j + 1) * half] for f in folded], axis=0)
            for j in range(NDIL)]
        values = softmax_back([s * scale for s in found], grad_prob)
        for j in range(count):
            prob_out[c, j] = pack(values[j])
        for j in range(NDIL):
            @pl.when(i >= 2**j)
            def _():
                prob_copy(j, c).start()
        stack = jnp.concatenate([v.astype(bf16) for v in values], axis=0)
        factor = dot_nn(stack, spread[:, :span])
        grads[0, c] = weighted(
            [factor[j * rows:(j + 1) * rows] for j in range(count)], sources)

        def last(first):
            part = dot_nn(rows_of(grads[0, pl.ds(first, batch)]), weights[0])
            total[pl.ds(first, batch)] = part.reshape(batch, rows, width)
        batched(c, last)

    def finish(c):
        for j in range(NDIL):
            @pl.when(i + 2**j < n)
            def _():
                prob_copy(j, c).wait_recv()
        packed = jnp.concatenate(
            [prob_out[c, 0], prob_in[c].reshape(NDIL * half, LANES)], axis=0)
        factor = dot_nn(packed, spread[...])
        for part in range(2):
            halves = []
            for h in range(2):
                at = slice(h * half, (h + 1) * half)
                cols = slice((2 * h + part) * span, (2 * h + part + 1) * span)
                halves.append(weighted(
                    [factor[j * half:(j + 1) * half, cols] for j in range(count)],
                    [back[c, part, at]] + [back_in[j, c, part, at] for j in range(NDIL)]))
            grads[1 + part, c] = jnp.concatenate(halves, axis=0)

        def last(first):
            put(0, first, functools.reduce(jnp.add, [
                dot_nn(rows_of(grads[x, pl.ds(first, batch)]), weights[x])
                for x in (1, 2)], rows_of(total[pl.ds(first, batch)])))
        batched(c, last)

    kinds = (FULL, BACK, KEYS)
    plan = (
        [(shifted(kind, 0), relay_far(kind)) for kind in kinds]
        + [(shifted(kind, SENT[kind]), functools.partial(direct, kind)) for kind in kinds]
        + [(shifted(kind, NEAR[kind]), relay_near(kind)) for kind in kinds]
        + [
            (shifted(FULL, MEET[FULL]), attend),
            (shifted(FULL, PART_NEAR), part_near),
            (shifted(FULL, PART_MID), part_mid),
            (shifted(BACK, MEET[BACK]), meet),
            (shifted(KEYS, MEET[KEYS]), soften),
            (shifted(KEYS, FINISH), finish),
            (shifted(FULL, COLLECT), collect),
        ])
    plan = [plan[x] for x in ORDER]
    steps = max(times[-1] for times, _ in plan) + 1

    def step(s, carry):
        for times, run in plan:
            late = [t for t in times if t >= 0]
            hit = functools.reduce(jnp.logical_or, [s == t for t in late])
            c = functools.reduce(
                jnp.add, [(s > t).astype(jnp.int32) for t in late]) + (len(times) - len(late))

            @pl.when(hit)
            def _():
                run(c)
        return carry

    lax.fori_loop(0, steps, step, 0)

    for kind in range(3):
        for way in range(6):
            copy, cond = hop(kind, way, ALL)

            @pl.when(cond)
            def _():
                copy.wait_send()
    for j in range(NDIL):
        for way, off, cond in returns(j):
            @pl.when(cond)
            def _():
                back_copy(j, way, off, ALL).wait_send()

        @pl.when(i >= 2**j)
        def _():
            prob_copy(j, ALL).wait_send()

        @pl.when(i + 2**j < n)
        def _():
            dot_copy(j, ALL).wait_send()
    for side in range(2):
        for c in range(0, chunks, batch):
            write(side, c).wait()


def per_device(queries, keys, values, grad_out, links, w_query, w_key, w_value):
    frames, patches, width = queries.shape
    n = lax.axis_size("frame")
    rows = 32
    chunks = patches // (2 * rows)
    half = rows // 2
    block = LANES
    span = HEADS * PIECE
    hbm = pl.BlockSpec(memory_space=pl.ANY)
    f32, bf16 = jnp.float32, jnp.bfloat16
    dma = pltpu.SemaphoreType.DMA
    one = (rows, width)
    return pl.pallas_call(
        functools.partial(kernel, n, chunks, rows),
        out_shape=jax.ShapeDtypeStruct((frames, patches, width), bf16),
        in_specs=[pl.BlockSpec(memory_space=pltpu.SMEM)] + [hbm] * 7,
        out_specs=hbm,
        scratch_shapes=[
            pltpu.VMEM((4, patches // block, block, width), bf16),
            pltpu.VMEM((chunks, 2) + one, bf16),
            pltpu.VMEM((chunks,) + one, bf16),
            pltpu.VMEM((chunks, 2) + one, bf16),
            pltpu.VMEM((chunks, 2) + one, bf16),
            pltpu.VMEM((chunks,) + one, bf16),
            pltpu.VMEM((NDIL, chunks, 2) + one, bf16),
            pltpu.VMEM((NDIL, chunks) + one, bf16),
            pltpu.VMEM((NDIL, chunks, 2) + one, bf16),
            pltpu.VMEM((NDIL, chunks) + one, bf16),
            pltpu.VMEM((6, chunks) + one, bf16),
            pltpu.VMEM((chunks, NDIL + 1, half, LANES), bf16),
            pltpu.VMEM((chunks, NDIL, half, LANES), bf16),
            pltpu.VMEM((chunks, NDIL, half, LANES), bf16),
            pltpu.VMEM((chunks, NDIL, half, LANES), bf16),
            pltpu.VMEM((chunks, rows, LANES), f32),
            pltpu.VMEM((chunks,) + one, f32),
            pltpu.VMEM((chunks,) + one, f32),
            pltpu.VMEM((chunks,) + one, f32),
            pltpu.VMEM((chunks,) + one, f32),
            pltpu.VMEM((4, chunks) + one, bf16),
            pltpu.VMEM((patches, width), bf16),
            pltpu.VMEM((4 * (NDIL + 1) * rows, span), bf16),
            pltpu.VMEM((span, LANES), bf16),
            pltpu.VMEM((LANES, 4 * span), bf16),
            pltpu.VMEM((2, LANES, LANES), bf16),
            pltpu.VMEM((3, width, width), bf16),
            pltpu.VMEM((3, width, width), bf16),
            dma((4, patches // block)),
            dma((3,)),
            dma((3, 6)),
            dma((3, NDIL, chunks)),
            dma((NDIL,)),
            dma((NDIL, chunks)),
            dma((NDIL,)),
            dma((NDIL, chunks)),
            dma((NDIL,)),
            dma((6, chunks)),
            dma((2, chunks)),
        ],
        compiler_params=pltpu.CompilerParams(
            collective_id=0, has_side_effects=True, vmem_limit_bytes=60 * 1024 * 1024),
    )(links, queries, keys, values, grad_out, w_query, w_key, w_value)


def solution(mesh):
    placed = (
        P(("dom", "frame"), None, None),
        P(("dom", "frame"), None, None),
        P(("dom", "frame"), None, None),
        P(("dom", "frame"), None, None),
        P(("dom", "frame"), None),
        P(),
        P(),
        P(),
    )
    return jax.shard_map(
        per_device,
        mesh=mesh,
        in_specs=placed,
        out_specs=P(("dom", "frame"), None, None),
        check_vma=False,
    )
```
